32 devices in a mesh: rows: 8 (over y, x, core), seq: 4 (over z).
Axes of the slice: x: 2, y: 2, z: 4, core: 2. Of those that a mesh axis runs over, the one named last changes fastest.
Arguments:
- tokens_in: bfloat16 [32, 4096, 512], P('rows', 'seq'), may hold values from -6 to 6
- layer_norm_gain: float32 [512], replicated, may hold values from 0.5 to 1.5
- layer_norm_bias: float32 [512], replicated, may hold values from -3 to 3
- input_real: bfloat16 [256, 512], replicated, may hold values from -0.1875 to 0.1875
- input_imag: bfloat16 [256, 512], replicated, may hold values from -0.1875 to 0.1875
- decay_log: float32 [256], replicated, may hold values from -7.5 to -3
- angle_log: float32 [256], replicated, may hold values from -5 to 0.5
- scale_log: float32 [256], replicated, may hold values from -0.5 to 0.5
- output_real: bfloat16 [512, 256], replicated, may hold values from -0.375 to 0.375
- output_imag: bfloat16 [512, 256], replicated, may hold values from -0.375 to 0.375
- skip_gain: float32 [512], replicated, may hold values from -3 to 3
- glu_value: bfloat16 [512, 512], replicated, may hold values from -0.5 to 0.5
- glu_gate: bfloat16 [512, 512], replicated, may hold values from -0.25 to 0.25
- glu_bias: float32 [1024], replicated, may hold values from -3 to 3
- doc_lengths: int32 [32, 8], P('rows'), may hold values from 1 to 1024, 4096 in all within a row
- out_grad: bfloat16 [32, 4096, 512], P('rows', 'seq'), may hold values from -6 to 6
Outputs:
- block_out: bfloat16 [32, 4096, 512], P('rows', 'seq')
- input_grad: bfloat16 [32, 4096, 512], P('rows', 'seq')
- norm_gain_grad: float32 [512], replicated
- norm_shift_grad: float32 [512], replicated
- input_real_grad: float32 [256, 512], replicated
- input_imag_grad: float32 [256, 512], replicated
- decay_log_grad: float32 [256], replicated
- angle_log_grad: float32 [256], replicated
- scale_log_grad: float32 [256], replicated
- output_real_grad: float32 [512, 256], replicated
- output_imag_grad: float32 [512, 256], replicated
- skip_gain_grad: float32 [512], replicated
- glu_value_grad: float32 [512, 512], replicated
- glu_gate_grad: float32 [512, 512], replicated
- glu_bias_grad: float32 [1024], replicated
The draws below stay inside these ranges and needn't reach their ends.
Inputs may be any that keep to these rules, and one draw needn't show every extreme that they name: `doc_lengths`: each row's entries sum to 4096; the last entry is the row's trailing padding, the others are its documents' lengths in order.
All inputs are finite; a program needn't handle non-finite values.
Results may differ from the reference program's by a relative error of at most 0.014.
Values may be sent and summed in bfloat16 or wider, within the bound.
No kernel may reach another device: no remote copies, remote signals or barrier semaphores. Data moves between devices by JAX's collectives and lax.ppermute only.
A program may use at most 192 MiB of HBM per device.

```python
import math
import jax
import jax.numpy as jnp
import numpy as np
from jax import lax

H = 512
N = 256
DOCS = 8
ROWS = 32
LEN = 4096


def shard_levels(own_key, extent, cuts, least, top_value):
    def one(axis_at, shards_of):
        heights = jax.random.uniform(jax.random.fold_in(jax.random.fold_in(own_key, 6), axis_at), (shards_of,), jnp.float32, least / len(cuts), top_value / len(cuts))
        return jnp.repeat(jnp.exp(heights), extent[axis_at] // shards_of).reshape((-1,) + (1,) * (len(extent) - axis_at - 1))

    level = one(*cuts[0])
    for cut in cuts[1:]:
        level = level * one(*cut)
    return level


def profile(amount, total, reach, skew):
    loads = [(1 << 20) // math.isqrt(grade ** skew) + 1 for grade in range(2, amount + 1)]
    surplus, given = total - reach - (amount - 1), [1] * (amount - 1)
    while surplus > 0:
        candidates = [i for i in range(amount - 1) if given[i] < reach]
        pool, left = sum([loads[i] for i in candidates]), surplus
        for i in candidates:
            addition = min(reach - given[i], max(1, left * loads[i] // pool), surplus)
            given[i] = given[i] + addition
            surplus = surplus - addition
    return np.array([reach] + given)


def uneven(stream_key, amount, total, most, slope):
    if amount == 2:
        one = jax.random.randint(stream_key, (), max(1, total - most), min(most, total - 1) + 1)
        return jnp.stack([one, total - one])
    lengths = jnp.asarray(profile(amount, total, most, slope), jnp.int32)
    pairs = (amount - 1) // 2
    source_of, sink = lengths[1:1 + 2 * pairs:2], lengths[2:2 + 2 * pairs:2]
    room = jnp.minimum(source_of - 1, most - sink)
    moved = jax.random.randint(jax.random.fold_in(stream_key, 1), (pairs,), 0, 1 << 20) % (room + 1)
    lengths = lengths.at[1:1 + 2 * pairs:2].set(source_of - moved).at[2:2 + 2 * pairs:2].set(sink + moved)
    return lengths[jax.random.permutation(jax.random.fold_in(stream_key, 2), amount)]


def bell_draw(key, dims, scale, bound, pieces=(), kind=jnp.bfloat16):
    values = scale * jax.random.normal(key, dims, jnp.float32)
    if pieces:
        values = values * shard_levels(key, dims, pieces, -0.22, 0.18)
    return jnp.clip(values, -bound, bound).astype(kind)


def setup_inputs(seed: int = 0) -> dict:
    seeds = jax.random.split(jax.random.key(seed), 17)
    tokens_in = bell_draw(seeds[0], (ROWS, LEN, H), 1.0, 6.0, ((0, 8), (1, 4)))
    layer_norm_gain = jnp.clip(jax.random.uniform(seeds[1], (H,), jnp.float32, 0.5, 1.5), 0.5, 1.5)
    layer_norm_bias = bell_draw(seeds[2], (H,), 0.5, 3.0, (), jnp.float32)
    input_real = bell_draw(seeds[3], (N, H), (2 * H) ** -0.5, 0.1875)
    input_imag = bell_draw(seeds[4], (N, H), (2 * H) ** -0.5, 0.1875)
    decay_log = jnp.clip(jax.random.uniform(seeds[5], (N,), jnp.float32, -7.5, -3.0), -7.5, -3.0)
    angle_log = jnp.clip(jax.random.uniform(seeds[6], (N,), jnp.float32, -5.0, 0.5), -5.0, 0.5)
    scale_log = jnp.clip(jax.random.uniform(seeds[7], (N,), jnp.float32, -0.5, 0.5), -0.5, 0.5)
    output_real = bell_draw(seeds[8], (H, N), N ** -0.5, 0.375)
    output_imag = bell_draw(seeds[9], (H, N), N ** -0.5, 0.375)
    skip_gain = bell_draw(seeds[10], (H,), 0.5, 3.0, (), jnp.float32)
    glu_value = bell_draw(seeds[11], (H, H), (H // 4) ** -0.5, 0.5)
    glu_gate = bell_draw(seeds[12], (H, H), H ** -0.5, 0.25)
    glu_bias = bell_draw(seeds[13], (2 * H,), 0.5, 3.0, (), jnp.float32)
    doc_lengths = jax.vmap(lambda own: uneven(own, DOCS, LEN, LEN // 4, 2))(jax.random.split(seeds[14], ROWS)).reshape((ROWS, DOCS)).astype(jnp.int32)
    out_grad = bell_draw(seeds[15], (ROWS, LEN, H), 1.0, 6.0, ((0, 8), (1, 4)))
    return {"tokens_in": tokens_in, "layer_norm_gain": layer_norm_gain, "layer_norm_bias": layer_norm_bias, "input_real": input_real, "input_imag": input_imag, "decay_log": decay_log, "angle_log": angle_log, "scale_log": scale_log, "output_real": output_real, "output_imag": output_imag, "skip_gain": skip_gain, "glu_value": glu_value, "glu_gate": glu_gate, "glu_bias": glu_bias, "doc_lengths": doc_lengths, "out_grad": out_grad}


EPSILON = 1e-05
HIGH = lax.Precision.HIGHEST

@jax.custom_vjp
def low(v):
    return lax.optimization_barrier(v.astype(jnp.bfloat16)).astype(jnp.float32)

@jax.custom_vjp
def low_back(v):
    return v

def low_keep(v):
    return (low(v), None)

def low_pass(kept, grad):
    return (grad,)

def back_keep(v):
    return (v, None)

def back_low(kept, grad):
    return (low(grad),)
low.defvjp(low_keep, low_pass)
low_back.defvjp(back_keep, back_low)

def layer_norm(values, gain, shift):
    centered_input = values - lax.optimization_barrier(jnp.mean(values, axis=-1, keepdims=True))
    spread = lax.optimization_barrier(jnp.mean(centered_input * centered_input, axis=-1, keepdims=True))
    return centered_input * lax.rsqrt(spread + EPSILON) * gain + shift

def decay_terms(decay_log, angle_log, scale_log):
    rate = jnp.exp(decay_log)
    radius = jnp.exp(-rate)
    angle = jnp.exp(angle_log)
    scale = jnp.exp(scale_log) * jnp.sqrt(1.0 - jnp.exp(-2.0 * rate))
    return (radius * jnp.cos(angle), radius * jnp.sin(angle), scale)

def forward_row(row, keep, layer_norm_gain, layer_norm_bias, input_real, input_imag, decay_log, angle_log, scale_log, output_real, output_imag, skip_gain, glu_value, glu_gate, glu_bias):
    width = row.shape[-1]
    normed_output = layer_norm(row, layer_norm_gain, layer_norm_bias)
    normed_low = low(normed_output)
    decay_real, decay_imag, scale = decay_terms(decay_log, angle_log, scale_log)
    scaled_real = low(input_real * scale[:, None])
    scaled_imag = low(input_imag * scale[:, None])
    drive_real = low(low_back(jnp.dot(normed_low, scaled_real.T, precision=HIGH)))
    drive_imag = low(low_back(jnp.dot(normed_low, scaled_imag.T, precision=HIGH)))

    def advance(state, current):
        state_real, state_imag = state
        keep_now, push_real, push_imag = current
        new_real = keep_now * (decay_real * state_real - decay_imag * state_imag) + push_real
        new_imag = keep_now * (decay_real * state_imag + decay_imag * state_real) + push_imag
        return ((new_real, new_imag), (new_real, new_imag))
    anchor = jnp.zeros(decay_real.shape, jnp.float32)
    _, (state_real, state_imag) = lax.scan(advance, (anchor, anchor), (keep, drive_real, drive_imag))
    sent_real = low(low_back(state_real))
    sent_imag = low(low_back(state_imag))
    mixed = jnp.dot(sent_real, output_real.T, precision=HIGH) - jnp.dot(sent_imag, output_imag.T, precision=HIGH)
    mixed = low_back(mixed + skip_gain * normed_output)
    activated = low(jax.nn.gelu(mixed, approximate=False))
    value = low_back(jnp.dot(activated, glu_value, precision=HIGH) + glu_bias[:width])
    gate = low_back(jnp.dot(activated, glu_gate, precision=HIGH) + glu_bias[width:])
    return row + value * jax.nn.sigmoid(gate)

def reference(tokens_in, layer_norm_gain, layer_norm_bias, input_real, input_imag, decay_log, angle_log, scale_log, output_real, output_imag, skip_gain, glu_value, glu_gate, glu_bias, doc_lengths, out_grad):
    params = tuple((item.astype(jnp.float32) for item in (layer_norm_gain, layer_norm_bias, input_real, input_imag, decay_log, angle_log, scale_log, output_real, output_imag, skip_gain, glu_value, glu_gate, glu_bias)))
    places = jnp.arange(LEN, dtype=jnp.int32)
    starts = (jnp.cumsum(doc_lengths, axis=1) - doc_lengths).astype(jnp.int32)
    hits = jnp.any(places[None, :, None] == starts[:, None, :], axis=-1)
    keep_all = jnp.where(hits, 1.0, 1.0).astype(jnp.float32) * jnp.where(hits, 0.0, 1.0).astype(jnp.float32)
    limit = (LEN - doc_lengths[:, -1]).astype(jnp.int32)
    valid_all = jnp.where(places[None, :] < limit[:, None], 1.0, 0.0).astype(jnp.float32)

    def per_row(totals, current):
        row, keep, valid, grad_row = current

        def apply(row_value, *weights):
            return forward_row(row_value, keep, *weights)
        result, pull = jax.vjp(apply, row.astype(jnp.float32), *params)
        pulled = pull(grad_row.astype(jnp.float32) * valid[:, None])
        totals = tuple((first + second for first, second in zip(totals, pulled[1:])))
        return (totals, (result.astype(jnp.bfloat16), pulled[0].astype(jnp.bfloat16)))
    zeros = tuple((jnp.zeros_like(item) for item in params))
    totals, (block_out, input_grad) = lax.scan(per_row, zeros, (tokens_in, keep_all, valid_all, out_grad))
    return (block_out, input_grad, totals[0], totals[1], totals[2], totals[3], totals[4], totals[5], totals[6], totals[7], totals[8], totals[9], totals[10], totals[11], totals[12])
```

```python
import functools

import jax
import jax.numpy as jnp
from jax import lax
from jax.experimental import pallas as pl
from jax.experimental.pallas import tpu as pltpu
from jax.sharding import PartitionSpec as P

EPSILON = 1e-05
SEGMENTS = 16
SUBLANES = 8
LANES = 128
F32 = jnp.float32
BF16 = jnp.bfloat16
VMEM_LIMIT = 60 * 1024 * 1024


def nt_dot(left, right):
    return lax.dot_general(
        left, right, (((1,), (1,)), ((), ())), preferred_element_type=F32
    )


def nn_dot(left, right):
    return lax.dot_general(
        left, right, (((1,), (0,)), ((), ())), preferred_element_type=F32
    )


def tn_dot(left, right):
    return lax.dot_general(
        left, right, (((0,), (0,)), ((), ())), preferred_element_type=F32
    )


def rows_of(step, half, span):
    return pl.ds(step + half * SUBLANES * span, SUBLANES, stride=span)


def fill_keep(lens_ref, row, shift, keep, segs, span):
    toks = keep.shape[0]
    docs = lens_ref.shape[1]
    keep[...] = jnp.ones_like(keep)
    segs[...] = jnp.ones_like(segs)
    start = -shift
    for j in range(docs):

        @pl.when((start >= 0) & (start < toks))
        def _(start=start):
            keep[pl.ds(start, 1), :] = jnp.zeros((1, keep.shape[1]), F32)
            segs[pl.ds(start // span, 1), :] = jnp.zeros((1, segs.shape[1]), F32)

        start = start + lens_ref[row, j]


def power_of(real, imag, times):
    while times > 1:
        real, imag = real * real - imag * imag, 2.0 * real * imag
        times //= 2
    return real, imag


def to_blocks(work, part, value):
    for b in range(work.shape[0]):
        work[b, part, :] = value[:, b * LANES : (b + 1) * LANES]


def from_blocks(work, part):
    return jnp.concatenate([work[b, part, :] for b in range(work.shape[0])], axis=1)


def lane_blocks(vector, sign=1.0):
    n = vector.shape[1]
    return [
        jnp.broadcast_to(sign * vector[:, b * LANES : (b + 1) * LANES], (SUBLANES, LANES))
        for b in range(n // LANES)
    ]


def segment_ends(work, keep, real, imag, ends, span, reverse):
    groups = SEGMENTS // SUBLANES
    half = len(real)
    n = half * LANES
    zero = jnp.zeros((SUBLANES, LANES), F32)

    def body(i, carry):
        t = span - 1 - i if reverse else i
        out = []
        at = 0
        for g in range(groups):
            rows = rows_of(t, g, span)
            k = keep[rows, :]
            for b in range(half):
                sr, si = carry[at], carry[at + 1]
                at += 2
                ar, ai = k * real[b], k * imag[b]
                out.append((ar * sr + work[b, rows, :]) - ai * si)
                out.append((ar * si + work[half + b, rows, :]) + ai * sr)
        return tuple(out)

    final = lax.fori_loop(0, span, body, (zero,) * (2 * groups * half), unroll=4)
    at = 0
    for g in range(groups):
        for b in range(half):
            lanes = slice(b * LANES, (b + 1) * LANES)
            ends[g * SUBLANES : (g + 1) * SUBLANES, lanes] = final[at]
            lanes = slice(n + b * LANES, n + (b + 1) * LANES)
            ends[g * SUBLANES : (g + 1) * SUBLANES, lanes] = final[at + 1]
            at += 2


def starting_states(inits, half):
    n = half * LANES
    begin = []
    for g in range(SEGMENTS // SUBLANES):
        for b in range(half):
            for base in (0, n):
                lanes = slice(base + b * LANES, base + (b + 1) * LANES)
                begin.append(inits[g * SUBLANES : (g + 1) * SUBLANES, lanes])
    return tuple(begin)


def compose_segments(ends, segs, real, imag, span, start_real, start_imag, inits, reverse):
    n = real.shape[1]
    pr, pi = power_of(real, imag, span)
    cr, ci = start_real, start_imag
    order = range(SEGMENTS - 1, -1, -1) if reverse else range(SEGMENTS)
    for s in order:
        if inits is not None:
            inits[s : s + 1, 0:n] = cr
            inits[s : s + 1, n : 2 * n] = ci
        k = segs[s : s + 1, :]
        ar, ai = k * pr, k * pi
        er, ei = ends[s : s + 1, 0:n], ends[s : s + 1, n : 2 * n]
        cr, ci = (ar * cr + er) - ai * ci, (ar * ci + ei) + ai * cr
    return cr, ci


def forward_kernel(
    lens, first, x_ref, gain, bias, scaled, lam, drive_ref, xhat_ref, rstd_ref, ends_ref,
    fin_ref, work, keep, segs
):
    row = pl.program_id(0)
    toks = x_ref.shape[1]
    n = lam.shape[1]
    span = toks // SEGMENTS
    fill_keep(lens, row, first[0], keep, segs, span)
    chunk = 256
    for c in range(toks // chunk):
        part = slice(c * chunk, (c + 1) * chunk)
        x = x_ref[0, part, :].astype(F32)
        cent = x - jnp.mean(x, axis=-1, keepdims=True)
        rstd = lax.rsqrt(jnp.mean(cent * cent, axis=-1, keepdims=True) + EPSILON)
        xhat = cent * rstd
        rstd_ref[0, part, :] = jnp.broadcast_to(rstd, (chunk, rstd_ref.shape[2]))
        xhat_ref[0, part, :] = xhat.astype(BF16)
        low = (xhat * gain[...] + bias[...]).astype(BF16)
        drive = nt_dot(low, scaled[...]).astype(BF16)
        drive_ref[0, part, :] = drive
        to_blocks(work, part, drive.astype(F32))
    real, imag = lam[0:1, :], lam[1:2, :]
    ends = ends_ref.at[0]
    segment_ends(work, keep, lane_blocks(real), lane_blocks(imag), ends, span, False)
    zero = jnp.zeros((1, n), F32)
    cr, ci = compose_segments(ends, segs, real, imag, span, zero, zero, None, False)
    fin_ref[0, :, 0:n] = cr
    fin_ref[0, :, n : 2 * n] = ci


TAIL_P = 0.3275911 * 0.7071067811865476
TAIL = (0.254829592, -0.284496736, 1.421413741, -1.453152027, 1.061405429)


def gelu_parts(m):
    bell = jnp.exp(-0.5 * m * m)
    t = 1.0 / (1.0 + TAIL_P * jnp.abs(m))
    poly = t * (0.5 * TAIL[0] + t * (0.5 * TAIL[1] + t * (0.5 * TAIL[2] + t * (0.5 * TAIL[3] + t * (0.5 * TAIL[4])))))
    tail = poly * bell
    return jnp.where(m < 0, tail, 1.0 - tail), bell


def middle_kernel(
    lens, first, drive_ref, ends_ref, carry_ref, xhat_ref, x_ref, og_ref, lam, out_cat, gain,
    bias, skip, wv, wg, gbias, block_ref, gm_ref, gs_ref, st_ref, bends_ref, bfin_ref, wglu_ref,
    wout_ref, gbias_ref, sums_ref, work, keep, segs, inits, act_s, gvg_s
):
    row = pl.program_id(0)
    toks, width = x_ref.shape[1], x_ref.shape[2]
    n = lam.shape[1]
    span = toks // SEGMENTS
    groups = SEGMENTS // SUBLANES

    @pl.when(row == 0)
    def _():
        wglu_ref[...] = jnp.zeros_like(wglu_ref)
        wout_ref[...] = jnp.zeros_like(wout_ref)
        gbias_ref[...] = jnp.zeros_like(gbias_ref)
        sums_ref[...] = jnp.zeros_like(sums_ref)

    fill_keep(lens, row, first[0], keep, segs, span)
    everything = slice(0, toks)
    to_blocks(work, everything, drive_ref[0].astype(F32))
    real, imag = lam[0:1, :], lam[1:2, :]
    half = n // LANES
    real_b, imag_b = lane_blocks(real), lane_blocks(imag)
    compose_segments(
        ends_ref.at[0], segs, real, imag, span, carry_ref[0, :, 0:n],
        carry_ref[0, :, n : 2 * n], inits, False
    )

    def body(t, carry):
        out = []
        at = 0
        for g in range(groups):
            rows = rows_of(t, g, span)
            k = keep[rows, :]
            for b in range(half):
                sr, si = carry[at], carry[at + 1]
                at += 2
                ar, ai = k * real_b[b], k * imag_b[b]
                nr = (ar * sr + work[b, rows, :]) - ai * si
                ni = (ar * si + work[half + b, rows, :]) + ai * sr
                work[b, rows, :] = nr
                work[half + b, rows, :] = ni
                out += [nr, ni]
        return tuple(out)

    lax.fori_loop(0, span, body, starting_states(inits, half), unroll=4)

    docs = lens.shape[1]
    limit = -first[0]
    for j in range(docs - 1):
        limit = limit + lens[row, j]
    chunk = 256
    ones = jnp.ones((SUBLANES, chunk), BF16)

    @pl.loop(0, toks // chunk)
    def _(c):
        part = pl.ds(pl.multiple_of(c * chunk, chunk), chunk)
        state = from_blocks(work, part).astype(BF16)
        st_ref[0, part, :] = state
        xhat = xhat_ref[0, part, :].astype(F32)
        mixed = nt_dot(state, out_cat[...]) + (xhat * (gain[...] * skip[...]) + bias[...] * skip[...])
        cdf, bell = gelu_parts(mixed)
        act = (mixed * cdf).astype(BF16)
        act_s[part, :] = act
        slope = cdf + mixed * (bell * 0.3989422804014327)
        value = nn_dot(act, wv[...]) + gbias[:, 0:width]
        gate = nn_dot(act, wg[...]) + gbias[:, width : 2 * width]
        sigma = 0.5 * jnp.tanh(0.5 * gate) + 0.5
        gated = value * sigma
        block_ref[0, part, :] = (x_ref[0, part, :].astype(F32) + gated).astype(BF16)
        place = lax.broadcasted_iota(jnp.int32, (chunk, width), 0) + c * chunk
        grad = jnp.where(place < limit, og_ref[0, part, :].astype(F32), 0.0)
        gv = (grad * sigma).astype(BF16)
        gg = (grad * gated * (1.0 - sigma)).astype(BF16)
        gvg_s[part, 0:width] = gv
        gvg_s[part, width : 2 * width] = gg
        gbias_ref[0:1, 0:width] += jnp.sum(gv.astype(F32), axis=0, keepdims=True)
        gbias_ref[0:1, width : 2 * width] += jnp.sum(gg.astype(F32), axis=0, keepdims=True)
        gact = nt_dot(gv, wv[...]) + nt_dot(gg, wg[...])
        gm = (gact * slope).astype(BF16)
        gm_ref[0, part, :] = gm
        gmf = gm.astype(F32)
        sums_ref[0:1, :] += jnp.sum(gmf, axis=0, keepdims=True)
        sums_ref[1:2, :] += jnp.sum(gmf * xhat, axis=0, keepdims=True)
        gs = nn_dot(gm, out_cat[...]).astype(BF16)
        gs_ref[0, part, :] = gs
        to_blocks(work, part, gs.astype(F32))

    wglu_ref[...] += tn_dot(act_s[...], gvg_s[...])
    wout_ref[...] += tn_dot(gm_ref[0], st_ref[0])

    fill_keep(lens, row, first[0] + 1, keep, segs, span)
    bends = bends_ref.at[0]
    segment_ends(work, keep, real_b, lane_blocks(imag, -1.0), bends, span, True)
    zero = jnp.zeros((1, n), F32)
    cr, ci = compose_segments(bends, segs, real, -imag, span, zero, zero, None, True)
    bfin_ref[0, :, 0:n] = cr
    bfin_ref[0, :, n : 2 * n] = ci


def backward_kernel(
    lens, first, gs_ref, bends_ref, carry_ref, st_ref, xhat_ref, gm_ref, og_ref, rstd_ref, lam,
    scaled, gain, skip, ig_ref, wg_ref, col_ref, lamg_ref, work, state, keep, segs, inits
):
    row = pl.program_id(0)
    toks, width = xhat_ref.shape[1], xhat_ref.shape[2]
    n = lam.shape[1]
    span = toks // SEGMENTS
    groups = SEGMENTS // SUBLANES

    @pl.when(row == 0)
    def _():
        wg_ref[...] = jnp.zeros_like(wg_ref)
        col_ref[...] = jnp.zeros_like(col_ref)
        lamg_ref[...] = jnp.zeros_like(lamg_ref)

    fill_keep(lens, row, first[0] + 1, keep, segs, span)
    everything = slice(0, toks)
    to_blocks(work, everything, gs_ref[0].astype(F32))
    to_blocks(state, everything, st_ref[0].astype(F32))
    real, imag = lam[0:1, :], -lam[1:2, :]
    half = n // LANES
    real_b, imag_b = lane_blocks(real), lane_blocks(imag)
    compose_segments(
        bends_ref.at[0], segs, real, imag, span, carry_ref[0, :, 0:n],
        carry_ref[0, :, n : 2 * n], inits, True
    )
    n_states = 2 * groups * half

    def body(i, carry):
        t = span - 1 - i
        out = []
        tot = list(carry[n_states:])
        at = 0
        for g in range(groups):
            rows = rows_of(t, g, span)
            k = keep[rows, :]
            for b in range(half):
                sr, si = carry[at], carry[at + 1]
                at += 2
                ur, ui = k * sr, k * si
                nr = (real_b[b] * ur + work[b, rows, :]) - imag_b[b] * ui
                ni = (real_b[b] * ui + work[half + b, rows, :]) + imag_b[b] * ur
                work[b, rows, :] = nr
                work[half + b, rows, :] = ni
                hr, hi = state[b, rows, :], state[half + b, rows, :]
                tot[4 * b] = tot[4 * b] + (ur * hr + ui * hi)
                tot[4 * b + 1] = tot[4 * b + 1] + (ui * hr - ur * hi)
                tot[4 * b + 2] = tot[4 * b + 2] + nr
                tot[4 * b + 3] = tot[4 * b + 3] + ni
                out += [nr, ni]
        return tuple(out) + tuple(tot)

    zero8 = jnp.zeros((SUBLANES, LANES), F32)
    final = lax.fori_loop(
        0, span, body, starting_states(inits, half) + (zero8,) * (4 * half), unroll=2
    )
    tot = final[n_states:]
    for b in range(half):
        low_lanes = slice(b * LANES, (b + 1) * LANES)
        high_lanes = slice(n + b * LANES, n + (b + 1) * LANES)
        lamg_ref[:, low_lanes] += tot[4 * b]
        lamg_ref[:, high_lanes] += tot[4 * b + 1]
        col_ref[:, low_lanes] += tot[4 * b + 2]
        col_ref[:, high_lanes] += tot[4 * b + 3]

    docs = lens.shape[1]
    limit = -first[0]
    for j in range(docs - 1):
        limit = limit + lens[row, j]
    adj = from_blocks(work, everything).astype(BF16)
    wg_ref[...] += tn_dot(adj, xhat_ref[0])
    chunk = 256
    mix = gain[...] * skip[...]

    @pl.loop(0, toks // chunk)
    def _(c):
        part = pl.ds(pl.multiple_of(c * chunk, chunk), chunk)
        low = from_blocks(work, part).astype(BF16)
        xhat = xhat_ref[0, part, :].astype(F32)
        g = nn_dot(low, scaled[...]) * gain[...] + gm_ref[0, part, :].astype(F32) * mix
        place = lax.broadcasted_iota(jnp.int32, (chunk, width), 0) + c * chunk
        grad = jnp.where(place < limit, og_ref[0, part, :].astype(F32), 0.0)
        m1 = jnp.mean(g, axis=-1, keepdims=True)
        m2 = jnp.mean(g * xhat, axis=-1, keepdims=True)
        ig_ref[0, part, :] = (grad + rstd_ref[0, part, 0:1] * (g - m1 - xhat * m2)).astype(BF16)


def whole(shape):
    return pl.BlockSpec(shape, lambda r: (0,) * len(shape))


def per_row(*shape):
    return pl.BlockSpec((1,) + shape, lambda r: (r,) + (0,) * len(shape))


SCALARS = pl.BlockSpec(memory_space=pltpu.SMEM)


def carry_over(fin, through, axis, parts, hops, reverse):
    def shift(v):
        pairs = [(i, i + 1) for i in range(parts - 1)]
        if reverse:
            pairs = [(b, a) for a, b in pairs]
        return lax.ppermute(v, axis, pairs)

    if hops == 1:
        return shift(fin)
    n = fin.shape[-1] // 2
    total = shift(fin)
    for _ in range(hops - 1):
        tr, ti = through[..., :n], through[..., n:]
        sr, si = total[..., :n], total[..., n:]
        passed = jnp.concatenate([tr * sr - ti * si, tr * si + ti * sr], axis=-1)
        total = shift(fin + passed)
    return total


def all_sum(v):
    return lax.psum(v, ("rows", "seq"))


def body(
    tokens_in, layer_norm_gain, layer_norm_bias, input_real, input_imag, decay_log, angle_log,
    scale_log, output_real, output_imag, skip_gain, glu_value, glu_gate, glu_bias, doc_lengths,
    out_grad
):
    rows_here, toks, width = tokens_in.shape
    n = input_real.shape[0]
    parts = lax.axis_size("seq")
    seat = lax.axis_index("seq")
    length = toks * parts
    hops = max(1, (length // 4) // toks)
    first = (seat * toks).astype(jnp.int32).reshape(1)
    rate = jnp.exp(decay_log)
    radius = jnp.exp(-rate)
    angle = jnp.exp(angle_log)
    cosine, sine = jnp.cos(angle), jnp.sin(angle)
    norm_root = jnp.sqrt(1.0 - jnp.exp(-2.0 * rate))
    scale = jnp.exp(scale_log) * norm_root
    lam = jnp.stack([radius * cosine, radius * sine])
    inputs = jnp.concatenate([input_real, input_imag], axis=0).astype(F32)
    scale2 = jnp.concatenate([scale, scale])
    scaled = (inputs * scale2[:, None]).astype(BF16)
    out_cat = jnp.concatenate([output_real, -output_imag], axis=1)
    gain, bias, skip = layer_norm_gain[None], layer_norm_bias[None], skip_gain[None]
    gbias = glu_bias[None]
    params = pltpu.CompilerParams(
        dimension_semantics=("arbitrary",), vmem_limit_bytes=VMEM_LIMIT
    )
    act = per_row(toks, width)
    sds = jax.ShapeDtypeStruct
    big = sds((rows_here, toks, width), BF16)
    drive, xhat, rstd, ends, fin = pl.pallas_call(
        forward_kernel,
        grid=(rows_here,),
        in_specs=[SCALARS, SCALARS, act, whole((1, width)), whole((1, width)),
                  whole((2 * n, width)), whole((2, n))],
        out_specs=[per_row(toks, 2 * n), act, per_row(toks, 128), per_row(SEGMENTS, 2 * n),
                   per_row(1, 2 * n)],
        out_shape=[sds((rows_here, toks, 2 * n), BF16), big, sds((rows_here, toks, 128), F32),
                   sds((rows_here, SEGMENTS, 2 * n), F32), sds((rows_here, 1, 2 * n), F32)],
        scratch_shapes=[pltpu.VMEM((2 * n // LANES, toks, LANES), F32), pltpu.VMEM((toks, LANES), F32),
                        pltpu.VMEM((SEGMENTS, n), F32)],
        compiler_params=params,
        name="forward",
    )(doc_lengths, first, tokens_in, gain, bias, scaled, lam)

    through = None
    back_through = None
    if hops > 1:
        starts = jnp.cumsum(doc_lengths, axis=1) - doc_lengths
        here = (starts >= first[0]) & (starts < first[0] + toks)
        clear = jnp.where(jnp.any(here, axis=1), 0.0, 1.0).astype(F32)
        here_next = (starts >= first[0] + 1) & (starts < first[0] + toks + 1)
        clear_next = jnp.where(jnp.any(here_next, axis=1), 0.0, 1.0).astype(F32)
        far = jnp.exp(-rate * toks)
        fr, fi = power_of(lam[0], lam[1], toks)
        through = clear[:, None, None] * jnp.concatenate([fr, fi])[None, None]
        back_through = clear_next[:, None, None] * jnp.concatenate([fr, -fi])[None, None]
    carry = carry_over(fin, through, "seq", parts, hops, False)

    block_out, gm, gs, st, bends, bfin, wglu, wout, gbias_g, sums = pl.pallas_call(
        middle_kernel,
        grid=(rows_here,),
        in_specs=[SCALARS, SCALARS, per_row(toks, 2 * n), per_row(SEGMENTS, 2 * n),
                  per_row(1, 2 * n), act, act, act, whole((2, n)), whole((width, 2 * n)),
                  whole((1, width)), whole((1, width)), whole((1, width)),
                  whole((width, width)), whole((width, width)), whole((1, 2 * width))],
        out_specs=[act, act, per_row(toks, 2 * n), per_row(toks, 2 * n),
                   per_row(SEGMENTS, 2 * n), per_row(1, 2 * n), whole((width, 2 * width)),
                   whole((width, 2 * n)), whole((1, 2 * width)), whole((2, width))],
        out_shape=[big, big, sds((rows_here, toks, 2 * n), BF16),
                   sds((rows_here, toks, 2 * n), BF16), sds((rows_here, SEGMENTS, 2 * n), F32),
                   sds((rows_here, 1, 2 * n), F32), sds((width, 2 * width), F32),
                   sds((width, 2 * n), F32), sds((1, 2 * width), F32), sds((2, width), F32)],
        scratch_shapes=[pltpu.VMEM((2 * n // LANES, toks, LANES), F32), pltpu.VMEM((toks, LANES), F32),
                        pltpu.VMEM((SEGMENTS, n), F32), pltpu.VMEM((SEGMENTS, 2 * n), F32),
                        pltpu.VMEM((toks, width), BF16), pltpu.VMEM((toks, 2 * width), BF16)],
        compiler_params=params,
        name="middle",
    )(doc_lengths, first, drive, ends, carry, xhat, tokens_in, out_grad, lam, out_cat, gain,
      bias, skip, glu_value, glu_gate, gbias)

    back_carry = carry_over(bfin, back_through, "seq", parts, hops, True)

    input_grad, win, col, lamg = pl.pallas_call(
        backward_kernel,
        grid=(rows_here,),
        in_specs=[SCALARS, SCALARS, per_row(toks, 2 * n), per_row(SEGMENTS, 2 * n),
                  per_row(1, 2 * n), per_row(toks, 2 * n), act, act, act, per_row(toks, 128),
                  whole((2, n)), whole((2 * n, width)), whole((1, width)), whole((1, width))],
        out_specs=[act, whole((2 * n, width)), whole((SUBLANES, 2 * n)),
                   whole((SUBLANES, 2 * n))],
        out_shape=[big, sds((2 * n, width), F32), sds((SUBLANES, 2 * n), F32),
                   sds((SUBLANES, 2 * n), F32)],
        scratch_shapes=[pltpu.VMEM((2 * n // LANES, toks, LANES), F32), pltpu.VMEM((2 * n // LANES, toks, LANES), F32),
                        pltpu.VMEM((toks, LANES), F32), pltpu.VMEM((SEGMENTS, n), F32),
                        pltpu.VMEM((SEGMENTS, 2 * n), F32)],
        compiler_params=params,
        name="backward",
    )(doc_lengths, first, gs, bends, back_carry, st, xhat, gm, out_grad, rstd, lam, scaled, gain,
      skip)

    wglu, wout, gbias_g, sums, win, col, lamg = all_sum(
        (wglu, wout, gbias_g, sums, win, jnp.sum(col, axis=0), jnp.sum(lamg, axis=0))
    )
    scaled_f = scaled.astype(F32)
    gain_grad = jnp.sum(scaled_f * win, axis=0) + skip_gain * sums[1]
    shift_grad = jnp.sum(scaled_f * col[:, None], axis=0) + skip_gain * sums[0]
    skip_grad = layer_norm_gain * sums[1] + layer_norm_bias * sums[0]
    scaled_total = win * layer_norm_gain[None] + col[:, None] * layer_norm_bias[None]
    in_grad = scaled_total * scale2[:, None]
    per_state = jnp.sum(scaled_total * inputs, axis=1)
    scale_grad = per_state[:n] + per_state[n:]
    lr, li = lamg[:n], lamg[n:]
    radius_grad = lr * cosine + li * sine
    angle_grad = radius * (li * cosine - lr * sine) * angle
    decay_grad = (
        -radius_grad * radius * rate
        + scale_grad * jnp.exp(scale_log) * jnp.exp(-2.0 * rate) * rate / norm_root
    )
    return (
        block_out, input_grad, gain_grad, shift_grad, in_grad[:n], in_grad[n:], decay_grad,
        angle_grad, scale_grad * scale, wout[:, :n], -wout[:, n:], skip_grad,
        wglu[:, :width], wglu[:, width:], gbias_g[0]
    )


def solution(mesh):
    tokens = P("rows", "seq", None)
    placed = (tokens,) + (P(),) * 13 + (P("rows", None), tokens)
    return jax.shard_map(
        body, mesh=mesh, in_specs=placed, out_specs=(tokens, tokens) + (P(),) * 13,
        check_vma=False,
    )
```

```python
import functools

import jax
import jax.numpy as jnp
from jax import lax
from jax.experimental import pallas as pl
from jax.experimental.pallas import tpu as pltpu
from jax.sharding import PartitionSpec as P

EPSILON = 1e-05
SEGMENTS = 16
SUBLANES = 8
LANES = 128
EXTRA = 16
F32 = jnp.float32
BF16 = jnp.bfloat16
VMEM_LIMIT = 60 * 1024 * 1024
GLUE_LIMIT = 16 * 1024 * 1024


def nt_dot(left, right):
    return lax.dot_general(
        left, right, (((1,), (1,)), ((), ())), preferred_element_type=F32
    )


def nn_dot(left, right):
    return lax.dot_general(
        left, right, (((1,), (0,)), ((), ())), preferred_element_type=F32
    )


def tn_dot(left, right):
    return lax.dot_general(
        left, right, (((0,), (0,)), ((), ())), preferred_element_type=F32
    )


def skewed_scan(step, inits, extra, span, reverse, ends=False):
    groups = SEGMENTS // SUBLANES
    per_group = len(inits) // groups
    seat = lax.broadcasted_iota(jnp.int32, (SUBLANES, LANES), 0)
    order = SUBLANES - 1 - seat if reverse else seat
    last = span + SUBLANES - 2

    def rows(i):
        base = last - i if reverse else i
        return [pl.ds(base + g * SUBLANES * span, SUBLANES, stride=span - 1) for g in range(groups)]

    states = list(inits)
    for i in range(SUBLANES):
        if i:
            states = [jnp.where(order == i, x, y) for x, y in zip(inits, states)]
        states, extra = step(rows(i), states, extra, order <= i)

    def body(i, carry):
        return step(rows(i), *carry, None)

    states, extra = lax.fori_loop(SUBLANES, span - 1, body, (states, extra), unroll=5)
    final = states
    for i in range(span - 1, last + 1):
        states, extra = step(rows(i), states, extra, order >= i - span + 1)
        if ends:
            final = [jnp.where(order == i - span + 1, x, y) for x, y in zip(states, final)]
    return final if ends else extra


def fill_keep(lens_ref, row, shift, keep, segs, span):
    toks = keep.shape[0]
    docs = lens_ref.shape[1]
    keep[...] = jnp.ones_like(keep)
    segs[...] = jnp.ones_like(segs)
    start = -shift
    for j in range(docs):

        @pl.when((start >= 0) & (start < toks))
        def _(start=start):
            keep[pl.ds(start, 1), :] = jnp.zeros((1, keep.shape[1]), F32)
            segs[pl.ds(start // span, 1), :] = jnp.zeros((1, segs.shape[1]), F32)

        start = start + lens_ref[row, j]


def power_of(real, imag, times):
    while times > 1:
        real, imag = real * real - imag * imag, 2.0 * real * imag
        times //= 2
    return real, imag


def to_blocks(work, part, value):
    for b in range(work.shape[0]):
        work[b, part, :] = value[:, b * LANES : (b + 1) * LANES]


def from_blocks(work, part):
    return jnp.concatenate([work[b, part, :] for b in range(work.shape[0])], axis=1)


def lane_blocks(vector, sign=1.0):
    n = vector.shape[1]
    return [
        jnp.broadcast_to(sign * vector[:, b * LANES : (b + 1) * LANES], (SUBLANES, LANES))
        for b in range(n // LANES)
    ]


def segment_ends(work, keep, real, imag, ends, span, reverse):
    groups = SEGMENTS // SUBLANES
    half = len(real)
    n = half * LANES
    zero = jnp.zeros((SUBLANES, LANES), F32)

    def step(rows, states, extra, live):
        out = []
        at = 0
        for g in range(groups):
            k = keep[rows[g], :]
            for b in range(half):
                sr, si = states[at], states[at + 1]
                at += 2
                ar, ai = k * real[b], k * imag[b]
                out.append((ar * sr + work[b, rows[g], :]) - ai * si)
                out.append((ar * si + work[half + b, rows[g], :]) + ai * sr)
        return out, extra

    final = skewed_scan(step, [zero] * (2 * groups * half), [], span, reverse, ends=True)
    at = 0
    for g in range(groups):
        for b in range(half):
            lanes = slice(b * LANES, (b + 1) * LANES)
            ends[g * SUBLANES : (g + 1) * SUBLANES, lanes] = final[at]
            lanes = slice(n + b * LANES, n + (b + 1) * LANES)
            ends[g * SUBLANES : (g + 1) * SUBLANES, lanes] = final[at + 1]
            at += 2


def starting_states(inits, half):
    n = half * LANES
    begin = []
    for g in range(SEGMENTS // SUBLANES):
        for b in range(half):
            for base in (0, n):
                lanes = slice(base + b * LANES, base + (b + 1) * LANES)
                begin.append(inits[g * SUBLANES : (g + 1) * SUBLANES, lanes])
    return begin


def compose_segments(ends, segs, real, imag, span, start_real, start_imag, inits, reverse):
    n = real.shape[1]
    pr, pi = power_of(real, imag, span)
    cr, ci = start_real, start_imag
    order = range(SEGMENTS - 1, -1, -1) if reverse else range(SEGMENTS)
    for s in order:
        if inits is not None:
            inits[s : s + 1, 0:n] = cr
            inits[s : s + 1, n : 2 * n] = ci
        k = segs[s : s + 1, :]
        ar, ai = k * pr, k * pi
        er, ei = ends[s : s + 1, 0:n], ends[s : s + 1, n : 2 * n]
        cr, ci = (ar * cr + er) - ai * ci, (ar * ci + ei) + ai * cr
    return cr, ci


def forward_kernel(
    lens, first, x_ref, gain, bias, scaled, lam, drive_ref, xhat_ref, rstd_ref, ends_ref,
    fin_ref, work, keep, segs
):
    row = pl.program_id(0)
    toks = x_ref.shape[1]
    n = lam.shape[1]
    span = toks // SEGMENTS
    fill_keep(lens, row, first[0], keep, segs, span)
    chunk = 256
    for c in range(toks // chunk):
        part = slice(c * chunk, (c + 1) * chunk)
        x = x_ref[0, part, :].astype(F32)
        cent = x - jnp.mean(x, axis=-1, keepdims=True)
        rstd = lax.rsqrt(jnp.mean(cent * cent, axis=-1, keepdims=True) + EPSILON)
        xhat = cent * rstd
        rstd_ref[0, part, :] = jnp.broadcast_to(rstd, (chunk, rstd_ref.shape[2]))
        xhat_ref[0, part, :] = xhat.astype(BF16)
        low = (xhat * gain[...] + bias[...]).astype(BF16)
        drive = nt_dot(low, scaled[...]).astype(BF16)
        drive_ref[0, part, :] = drive
        to_blocks(work, part, drive.astype(F32))
    real, imag = lam[0:1, :], lam[1:2, :]
    ends = ends_ref.at[0]
    segment_ends(work, keep, lane_blocks(real), lane_blocks(imag), ends, span, False)
    zero = jnp.zeros((1, n), F32)
    cr, ci = compose_segments(ends, segs, real, imag, span, zero, zero, None, False)
    fin_ref[0, :, 0:n] = cr
    fin_ref[0, :, n : 2 * n] = ci


TAIL_P = 0.3275911 * 0.7071067811865476
TAIL = (0.254829592, -0.284496736, 1.421413741, -1.453152027, 1.061405429)


def gelu_parts(m):
    bell = jnp.exp(-0.5 * m * m)
    t = 1.0 / (1.0 + TAIL_P * jnp.abs(m))
    poly = t * (0.5 * TAIL[0] + t * (0.5 * TAIL[1] + t * (0.5 * TAIL[2] + t * (0.5 * TAIL[3] + t * (0.5 * TAIL[4])))))
    tail = poly * bell
    return jnp.where(m < 0, tail, 1.0 - tail), bell


def middle_kernel(
    lens, first, drive_ref, ends_ref, carry_ref, xhat_ref, x_ref, og_ref, lam, out_cat, gain,
    bias, skip, wv, wg, gbias, block_ref, gm_ref, gs_ref, st_ref, bends_ref, bfin_ref, mine_ref,
    send_ref, gbias_ref, sums_ref, work, keep, segs, done, inits, act_s, gvg_s, acc
):
    row = pl.program_id(0)
    toks, width = x_ref.shape[1], x_ref.shape[2]
    n = lam.shape[1]
    span = toks // SEGMENTS
    groups = SEGMENTS // SUBLANES

    @pl.when(row == 0)
    def _():
        acc[...] = jnp.zeros_like(acc)
        gbias_ref[...] = jnp.zeros_like(gbias_ref)
        sums_ref[...] = jnp.zeros_like(sums_ref)

    fill_keep(lens, row, first[0], keep, segs, span)
    everything = slice(0, toks)
    to_blocks(work, everything, drive_ref[0].astype(F32))
    real, imag = lam[0:1, :], lam[1:2, :]
    half = n // LANES
    real_b, imag_b = lane_blocks(real), lane_blocks(imag)
    compose_segments(
        ends_ref.at[0], segs, real, imag, span, carry_ref[0, :, 0:n],
        carry_ref[0, :, n : 2 * n], inits, False
    )

    def step(rows, states, extra, live):
        out = []
        at = 0
        for g in range(groups):
            k = keep[rows[g], :]
            for b in range(half):
                sr, si = states[at], states[at + 1]
                at += 2
                ar, ai = k * real_b[b], k * imag_b[b]
                nr = (ar * sr + work[b, rows[g], :]) - ai * si
                ni = (ar * si + work[half + b, rows[g], :]) + ai * sr
                done[b, rows[g], :] = nr
                done[half + b, rows[g], :] = ni
                out += [nr, ni]
        return out, extra

    skewed_scan(step, starting_states(inits, half), [], span, False)

    docs = lens.shape[1]
    limit = -first[0]
    for j in range(docs - 1):
        limit = limit + lens[row, j]
    chunk = 256
    ones = jnp.ones((SUBLANES, chunk), BF16)

    @pl.loop(0, toks // chunk)
    def _(c):
        part = pl.ds(pl.multiple_of(c * chunk, chunk), chunk)
        state = from_blocks(done, part).astype(BF16)
        st_ref[0, part, :] = state
        xhat = xhat_ref[0, part, :].astype(F32)
        mixed = nt_dot(state, out_cat[...]) + (xhat * (gain[...] * skip[...]) + bias[...] * skip[...])
        cdf, bell = gelu_parts(mixed)
        act = (mixed * cdf).astype(BF16)
        act_s[part, :] = act
        slope = cdf + mixed * (bell * 0.3989422804014327)
        value = nn_dot(act, wv[...]) + gbias[:, 0:width]
        gate = nn_dot(act, wg[...]) + gbias[:, width : 2 * width]
        sigma = 0.5 * jnp.tanh(0.5 * gate) + 0.5
        gated = value * sigma
        block_ref[0, part, :] = (x_ref[0, part, :].astype(F32) + gated).astype(BF16)
        place = lax.broadcasted_iota(jnp.int32, (chunk, width), 0) + c * chunk
        grad = jnp.where(place < limit, og_ref[0, part, :].astype(F32), 0.0)
        gv = (grad * sigma).astype(BF16)
        gg = (grad * gated * (1.0 - sigma)).astype(BF16)
        gvg_s[part, 0:width] = gv
        gvg_s[part, width : 2 * width] = gg
        gbias_ref[0:1, 0:width] += jnp.sum(gv.astype(F32), axis=0, keepdims=True)
        gbias_ref[0:1, width : 2 * width] += jnp.sum(gg.astype(F32), axis=0, keepdims=True)
        gact = nt_dot(gv, wv[...]) + nt_dot(gg, wg[...])
        gm = (gact * slope).astype(BF16)
        gm_ref[0, part, :] = gm
        gmf = gm.astype(F32)
        sums_ref[0:1, :] += jnp.sum(gmf, axis=0, keepdims=True)
        sums_ref[1:2, :] += jnp.sum(gmf * xhat, axis=0, keepdims=True)
        gs = nn_dot(gm, out_cat[...]).astype(BF16)
        gs_ref[0, part, :] = gs
        to_blocks(work, part, gs.astype(F32))

    acc[:, 0 : 2 * width] += tn_dot(act_s[...], gvg_s[...])
    acc[:, 2 * width :] += tn_dot(gm_ref[0], st_ref[0])

    fill_keep(lens, row, first[0] + 1, keep, segs, span)
    bends = bends_ref.at[0]
    segment_ends(work, keep, real_b, lane_blocks(imag, -1.0), bends, span, True)
    zero = jnp.zeros((1, n), F32)
    cr, ci = compose_segments(bends, segs, real, -imag, span, zero, zero, None, True)
    bfin_ref[0, :, 0:n] = cr
    bfin_ref[0, :, n : 2 * n] = ci

    @pl.when(row == pl.num_programs(0) - 1)
    def _():
        split_halves(acc, first[1], mine_ref, send_ref)


def split_halves(acc, core, mine_ref, send_ref):
    half = acc.shape[0] // 2
    mine_ref[0:half, :] = acc[pl.ds(pl.multiple_of(core * half, half), half), :].astype(BF16)
    send_ref[0:half, :] = acc[pl.ds(pl.multiple_of((1 - core) * half, half), half), :].astype(BF16)


def put_pair(vec, ref, at):
    high = vec.astype(BF16)
    low = (vec - high.astype(F32)).astype(BF16)
    ref[at : at + 2 * SUBLANES, :] = jnp.concatenate([high, low], axis=0)


def get_pair(ref, at):
    return (
        ref[at : at + SUBLANES, :].astype(F32)
        + ref[at + SUBLANES : at + 2 * SUBLANES, :].astype(F32)
    )


def adjoint_kernel(
    lens, first, gs_ref, bends_ref, carry_ref, st_ref, xhat_ref, lam, gbias_ref, sums_ref, adj_ref,
    mine_ref, send_ref, state, work, keep, segs, done, inits, acc, tots
):
    row = pl.program_id(0)
    toks, width = xhat_ref.shape[1], xhat_ref.shape[2]
    n = lam.shape[1]
    span = toks // SEGMENTS
    groups = SEGMENTS // SUBLANES

    @pl.when(row == 0)
    def _():
        acc[...] = jnp.zeros_like(acc)
        tots[...] = jnp.zeros_like(tots)

    fill_keep(lens, row, first[0] + 1, keep, segs, span)
    everything = slice(0, toks)
    to_blocks(work, everything, gs_ref[0].astype(F32))
    to_blocks(state, everything, st_ref[0].astype(F32))
    real, imag = lam[0:1, :], -lam[1:2, :]
    half = n // LANES
    real_b, imag_b = lane_blocks(real), lane_blocks(imag)
    compose_segments(
        bends_ref.at[0], segs, real, imag, span, carry_ref[0, :, 0:n],
        carry_ref[0, :, n : 2 * n], inits, True
    )

    def step(rows, states, tot, live):
        out = []
        tot = list(tot)
        at = 0
        for g in range(groups):
            k = keep[rows[g], :]
            for b in range(half):
                sr, si = states[at], states[at + 1]
                at += 2
                ur, ui = k * sr, k * si
                nr = (real_b[b] * ur + work[b, rows[g], :]) - imag_b[b] * ui
                ni = (real_b[b] * ui + work[half + b, rows[g], :]) + imag_b[b] * ur
                done[b, rows[g], :] = nr
                done[half + b, rows[g], :] = ni
                out += [nr, ni]
                hr, hi = state[b, rows[g], :], state[half + b, rows[g], :]
                if live is not None:
                    ur, ui, nr, ni = (jnp.where(live, v, 0.0) for v in (ur, ui, nr, ni))
                tot[4 * b] = tot[4 * b] + (ur * hr + ui * hi)
                tot[4 * b + 1] = tot[4 * b + 1] + (ui * hr - ur * hi)
                tot[4 * b + 2] = tot[4 * b + 2] + nr
                tot[4 * b + 3] = tot[4 * b + 3] + ni
        return out, tot

    zero8 = jnp.zeros((SUBLANES, LANES), F32)
    tot = skewed_scan(step, starting_states(inits, half), [zero8] * (4 * half), span, True)
    for b in range(half):
        low_lanes = slice(b * LANES, (b + 1) * LANES)
        high_lanes = slice(n + b * LANES, n + (b + 1) * LANES)
        tots[0, :, low_lanes] += tot[4 * b]
        tots[0, :, high_lanes] += tot[4 * b + 1]
        tots[1, :, low_lanes] += tot[4 * b + 2]
        tots[1, :, high_lanes] += tot[4 * b + 3]

    adj = from_blocks(done, everything).astype(BF16)
    adj_ref[0] = adj
    acc[...] += tn_dot(adj, xhat_ref[0])

    @pl.when(row == pl.num_programs(0) - 1)
    def _():
        split_halves(acc, first[1], mine_ref, send_ref)
        vec = jnp.concatenate(
            [gbias_ref[:, 0:width], gbias_ref[:, width : 2 * width], sums_ref[...],
             jnp.sum(tots[0], axis=0, keepdims=True), jnp.sum(tots[1], axis=0, keepdims=True),
             jnp.zeros((2, width), F32)], axis=0
        )
        put_pair(vec, mine_ref, n)
        put_pair(vec, send_ref, n)


def input_kernel(
    begin, lens, first, adj_ref, xhat_ref, gm_ref, og_ref, rstd_ref, scaled, gain, skip, *refs
):
    ig_ref = refs[-1]
    row = pl.program_id(0) + begin
    toks, width = xhat_ref.shape[1], xhat_ref.shape[2]
    docs = lens.shape[1]
    limit = -first[0]
    for j in range(docs - 1):
        limit = limit + lens[row, j]
    chunk = 256
    mix = gain[...] * skip[...]

    @pl.loop(0, toks // chunk)
    def _(c):
        part = pl.ds(pl.multiple_of(c * chunk, chunk), chunk)
        xhat = xhat_ref[0, part, :].astype(F32)
        g = nn_dot(adj_ref[0, part, :], scaled[...]) * gain[...]
        g = g + gm_ref[0, part, :].astype(F32) * mix
        place = lax.broadcasted_iota(jnp.int32, (chunk, width), 0) + c * chunk
        grad = jnp.where(place < limit, og_ref[0, part, :].astype(F32), 0.0)
        m1 = jnp.mean(g, axis=-1, keepdims=True)
        m2 = jnp.mean(g * xhat, axis=-1, keepdims=True)
        ig_ref[0, part, :] = (grad + rstd_ref[0, part, 0:1] * (g - m1 - xhat * m2)).astype(BF16)


def tree_sum(items):
    while len(items) > 1:
        items = [items[i] + items[i + 1] for i in range(0, len(items), 2)]
    return items[0]


def split_kernel(extra, place, mine_ref, got_ref, own_ref, *send_refs):
    half = mine_ref.shape[0] - extra
    piece = own_ref.shape[0] - extra

    def part(index):
        rows = pl.ds(pl.multiple_of(index * piece, piece), piece)
        return mine_ref[rows, :].astype(F32) + got_ref[rows, :].astype(F32)

    refs = (own_ref,) + send_refs
    for j, ref in enumerate(refs):
        ref[0:piece, :] = part(place[2] ^ j).astype(BF16)
    if extra:
        vec = get_pair(mine_ref, half) + get_pair(got_ref, half)
        for ref in refs:
            put_pair(vec, ref, piece)


def sum_kernel(extra, *refs):
    out = refs[-1]
    rows = out.shape[0] - extra
    out[0:rows, :] = tree_sum([r[0:rows, :].astype(F32) for r in refs[:-1]]).astype(BF16)
    if extra:
        put_pair(tree_sum([get_pair(r, rows) for r in refs[:-1]]), out, rows)


def gather_kernel(place, own_ref, *refs):
    out_ref = refs[-1]
    piece = refs[0].shape[0]
    for j, ref in enumerate((own_ref,) + refs[:-1]):
        rows = pl.ds(pl.multiple_of((place[2] ^ j) * piece, piece), piece)
        out_ref[rows, :] = ref[0:piece, :]


def weights_kernel(place, mine_ref, got_ref, value_ref, gate_ref, real_ref, imag_ref):
    width = value_ref.shape[1]
    n = real_ref.shape[1]
    total = jnp.where(pl.program_id(0) == 0, mine_ref[...], got_ref[...]).astype(F32)
    value_ref[...] = total[:, 0:width]
    gate_ref[...] = total[:, width : 2 * width]
    real_ref[...] = total[:, 2 * width : 2 * width + n]
    imag_ref[...] = -total[:, 2 * width + n :]


def exact_dot(left, right, dims):
    return lax.dot_general(
        left, right, (dims, ((), ())), precision=lax.Precision.HIGHEST, preferred_element_type=F32
    )


def last_kernel(
    place, mine_ref, got_ref, own_ref, scaled_ref, real_ref, imag_ref, scale_ref, gain, bias, skip,
    real_out, imag_out, small_out
):
    n, width = real_ref.shape
    vec = get_pair(own_ref, own_ref.shape[0] - 2 * SUBLANES)
    sum_gm, sum_gmx = vec[2:3, :], vec[3:4, :]
    col = jnp.broadcast_to(vec[5:6, :], (SUBLANES, 2 * n))
    lead = lax.broadcasted_iota(jnp.int32, (SUBLANES, width), 0) == 0
    spread = exact_dot(jnp.where(lead, col, 0.0), jnp.broadcast_to(bias[...], (SUBLANES, width)),
                       ((0,), (0,)))
    ones = jnp.ones((SUBLANES, width), F32)
    shift = exact_dot(col, scaled_ref[...].astype(F32), ((1,), (0,)))
    gain_sum = jnp.zeros((1, width), F32)
    scale_grad = jnp.zeros((SUBLANES, n), F32)
    first_core = place[1] == 0
    for part, weight_ref, out_ref in ((0, real_ref, real_out), (1, imag_ref, imag_out)):
        rows = slice(part * n, (part + 1) * n)
        keep_mine = first_core if part == 0 else jnp.logical_not(first_core)
        total = jnp.where(keep_mine, mine_ref[...], got_ref[...]).astype(F32)
        gain_sum = gain_sum + jnp.sum(total * scaled_ref[rows, :].astype(F32), axis=0, keepdims=True)
        full = total * gain[...] + spread[rows, :]
        out_ref[...] = full * scale_ref[rows, 0:1]
        scale_grad = scale_grad + exact_dot(ones, full * weight_ref[...].astype(F32), ((1,), (1,)))
    small_out[0:1, :] = gain_sum + skip[...] * sum_gmx
    small_out[1:2, :] = shift[0:1, :] + skip[...] * sum_gm
    small_out[2:3, :] = gain[...] * sum_gmx + bias[...] * sum_gm
    small_out[3:4, :] = jnp.concatenate([scale_grad[0:1, :]] * 2, axis=1)
    small_out[4:5, :] = vec[4:5, :]
    small_out[5:7, :] = vec[0:2, :]
    small_out[7:8, :] = jnp.zeros((1, width), F32)


def whole(shape):
    return pl.BlockSpec(shape, lambda r: (0,) * len(shape))


def per_row(*shape):
    return pl.BlockSpec((1,) + shape, lambda r: (r,) + (0,) * len(shape))


SCALARS = pl.BlockSpec(memory_space=pltpu.SMEM)


def carry_over(fin, through, axis, parts, hops, reverse):
    def shift(v):
        pairs = [(i, i + 1) for i in range(parts - 1)]
        if reverse:
            pairs = [(b, a) for a, b in pairs]
        return lax.ppermute(v, axis, pairs)

    if hops == 1:
        return shift(fin)
    n = fin.shape[-1] // 2
    total = shift(fin)
    for _ in range(hops - 1):
        tr, ti = through[..., :n], through[..., n:]
        sr, si = total[..., :n], total[..., n:]
        passed = jnp.concatenate([tr * sr - ti * si, tr * si + ti * sr], axis=-1)
        total = shift(fin + passed)
    return total


def glue(kernel, outs, *args, name, scalars=True):
    def spec(v):
        return pl.BlockSpec(v.shape, lambda i: (0,) * len(v.shape))

    specs = [SCALARS] * scalars + [spec(v) for v in args[scalars:]]
    many = isinstance(outs, list)
    return pl.pallas_call(
        kernel, grid=(1,), in_specs=specs, out_specs=[spec(v) for v in outs] if many else spec(outs),
        out_shape=outs, cost_estimate=cost(1.7),
        compiler_params=pltpu.CompilerParams(vmem_limit_bytes=GLUE_LIMIT), name=name,
    )(*args)


def from_core(v):
    return lax.ppermute(v, "rows", [(i, i ^ 1) for i in range(lax.axis_size("rows"))])


def from_plane(v, offset):
    count = lax.axis_size("rows")
    return lax.ppermute(v, "rows", [(i, i ^ (2 * offset)) for i in range(count)])


def from_line(v, offset):
    return lax.ppermute(v, "seq", [(i, i ^ offset) for i in range(lax.axis_size("seq"))])


def after(v, *others):
    return lax.optimization_barrier((v,) + others)[0]


class Exchange:
    def __init__(self, place, mine, send, extra, name):
        self.place, self.mine, self.extra, self.name = place, mine, extra, name
        self.plane = lax.axis_size("rows") // 2
        self.line = lax.axis_size("seq")
        self.half, self.cols = mine.shape[0] - extra, mine.shape[1]
        self.piece = SDS((self.half // self.plane + extra, self.cols), BF16)
        self.got = [from_core(send)]

    def split(self, place):
        self.own, *cuts = glue(
            functools.partial(split_kernel, self.extra), [self.piece] * self.plane, place,
            self.mine, *self.got, name=self.name + "_split"
        )
        self.got = [from_plane(c, j + 1) for j, c in enumerate(cuts)]
        return self.own

    def add(self, step, own=None):
        return glue(
            functools.partial(sum_kernel, self.extra), self.piece,
            self.own if own is None else own, *self.got, name=self.name + step, scalars=False
        )

    def add_plane(self, own=None):
        self.own = self.add("_plane", own)
        self.got = [from_line(self.own, j) for j in range(1, self.line)]
        return self.own

    def add_line(self, own=None):
        self.own = self.add("_line", own)
        total = self.own[: self.half // self.plane] if self.extra else self.own
        self.got = [from_plane(total, j) for j in range(1, self.plane)]
        return self.own

    def gather(self, place):
        self.mine = glue(
            gather_kernel, SDS((self.half, self.cols), BF16), place, self.own, *self.got,
            name=self.name + "_gather"
        )
        self.got = [from_core(self.mine)]
        return self.mine


def cost(us):
    return pl.CostEstimate(flops=int(us * 1e9), bytes_accessed=1 << 20, transcendentals=0)


PARAMS = pltpu.CompilerParams(
    dimension_semantics=("arbitrary",), vmem_limit_bytes=VMEM_LIMIT
)
SDS = jax.ShapeDtypeStruct


def scan_scratch(toks, n):
    return [
        pltpu.VMEM((2 * n // LANES, toks, LANES), F32), pltpu.VMEM((toks, LANES), F32),
        pltpu.VMEM((SEGMENTS, n), F32),
    ]


def run_forward(lens, place, x, gain, bias, scaled, lam):
    rows_here, toks, width = x.shape
    n = lam.shape[1]
    act = per_row(toks, width)
    return pl.pallas_call(
        forward_kernel,
        grid=(rows_here,),
        in_specs=[SCALARS, SCALARS, act, whole((1, width)), whole((1, width)),
                  whole((2 * n, width)), whole((2, n))],
        out_specs=[per_row(toks, 2 * n), act, per_row(toks, 128), per_row(SEGMENTS, 2 * n),
                   per_row(1, 2 * n)],
        out_shape=[SDS((rows_here, toks, 2 * n), BF16), SDS(x.shape, BF16),
                   SDS((rows_here, toks, 128), F32), SDS((rows_here, SEGMENTS, 2 * n), F32),
                   SDS((rows_here, 1, 2 * n), F32)],
        scratch_shapes=scan_scratch(toks, n),
        compiler_params=PARAMS,
        cost_estimate=cost(10.6),
        name="forward",
    )(lens, place, x, gain, bias, scaled, lam)


def run_middle(
    lens, place, drive, ends, carry, xhat, x, og, lam, out_cat, gain, bias, skip, wv, wg, gbias
):
    rows_here, toks, width = x.shape
    n = lam.shape[1]
    cols = 2 * width + 2 * n
    act, chan = per_row(toks, width), per_row(toks, 2 * n)
    return pl.pallas_call(
        middle_kernel,
        grid=(rows_here,),
        in_specs=[SCALARS, SCALARS, chan, per_row(SEGMENTS, 2 * n),
                  per_row(1, 2 * n), act, act, act, whole((2, n)), whole((width, 2 * n)),
                  whole((1, width)), whole((1, width)), whole((1, width)),
                  whole((width, width)), whole((width, width)), whole((1, 2 * width))],
        out_specs=[act, act, chan, chan, per_row(SEGMENTS, 2 * n), per_row(1, 2 * n),
                   whole((width // 2, cols)), whole((width // 2, cols)), whole((1, 2 * width)),
                   whole((2, width))],
        out_shape=[SDS(x.shape, BF16), SDS(x.shape, BF16), SDS((rows_here, toks, 2 * n), BF16),
                   SDS((rows_here, toks, 2 * n), BF16), SDS((rows_here, SEGMENTS, 2 * n), F32),
                   SDS((rows_here, 1, 2 * n), F32), SDS((width // 2, cols), BF16),
                   SDS((width // 2, cols), BF16), SDS((1, 2 * width), F32),
                   SDS((2, width), F32)],
        scratch_shapes=scan_scratch(toks, n) + [
            pltpu.VMEM((2 * n // LANES, toks, LANES), F32), pltpu.VMEM((SEGMENTS, 2 * n), F32),
            pltpu.VMEM((toks, width), BF16),
            pltpu.VMEM((toks, 2 * width), BF16), pltpu.VMEM((width, cols), F32)],
        compiler_params=PARAMS,
        cost_estimate=cost(48),
        name="middle",
    )(lens, place, drive, ends, carry, xhat, x, og, lam, out_cat, gain, bias, skip, wv, wg, gbias)


def run_adjoint(lens, place, gs, bends, carry, st, xhat, lam, gbias_g, sums):
    rows_here, toks, width = xhat.shape
    n = lam.shape[1]
    act, chan = per_row(toks, width), per_row(toks, 2 * n)
    return pl.pallas_call(
        adjoint_kernel,
        grid=(rows_here,),
        in_specs=[SCALARS, SCALARS, chan, per_row(SEGMENTS, 2 * n), per_row(1, 2 * n), chan, act,
                  whole((2, n)), whole((1, 2 * width)), whole((2, width))],
        out_specs=[chan, whole((n + EXTRA, width)), whole((n + EXTRA, width))],
        out_shape=[SDS((rows_here, toks, 2 * n), BF16), SDS((n + EXTRA, width), BF16),
                   SDS((n + EXTRA, width), BF16)],
        scratch_shapes=[pltpu.VMEM((2 * n // LANES, toks, LANES), F32)] + scan_scratch(toks, n) + [
            pltpu.VMEM((2 * n // LANES, toks, LANES), F32), pltpu.VMEM((SEGMENTS, 2 * n), F32),
            pltpu.VMEM((2 * n, width), F32),
            pltpu.VMEM((2, SUBLANES, 2 * n), F32)],
        compiler_params=PARAMS,
        cost_estimate=cost(12),
        name="adjoint",
    )(lens, place, gs, bends, carry, st, xhat, lam, gbias_g, sums)


def run_input(lens, place, adj, xhat, gm, og, rstd, scaled, gain, skip, begin=0, end=None, into=None):
    rows_here, toks, width = xhat.shape
    end = rows_here if end is None else end

    def rows(*shape):
        return pl.BlockSpec((1,) + shape, lambda r: (r + begin if begin else r, 0, 0))

    act = rows(toks, width)
    args = (lens, place, adj, xhat, gm, og, rstd, scaled, gain, skip)
    specs = [SCALARS, SCALARS, rows(toks, adj.shape[2]), act, act, act,
             rows(toks, 128), whole(scaled.shape), whole((1, width)), whole((1, width))]
    if into is not None:
        args, specs = args + (into,), specs + [pl.BlockSpec(memory_space=pl.ANY)]
    return pl.pallas_call(
        functools.partial(input_kernel, begin),
        grid=(end - begin,),
        in_specs=specs,
        out_specs=act,
        out_shape=SDS(xhat.shape, BF16),
        input_output_aliases={} if into is None else {len(args) - 1: 0},
        compiler_params=PARAMS,
        cost_estimate=cost(8),
        name="input",
    )(*args)


def run_weights(place, mine, got, width, n):
    half, cols = mine.shape
    blocks = 2
    tall = half // blocks
    source = pl.BlockSpec((tall, cols), lambda p, i, place: (i, 0))

    def out(c):
        return pl.BlockSpec((tall, c), lambda p, i, place: ((place[1] ^ p) * blocks + i, 0))

    return pl.pallas_call(
        weights_kernel,
        grid_spec=pltpu.PrefetchScalarGridSpec(
            num_scalar_prefetch=1, grid=(2, blocks), in_specs=[source, source],
            out_specs=[out(width), out(width), out(n), out(n)],
        ),
        out_shape=[SDS((2 * half, width), F32)] * 2 + [SDS((2 * half, n), F32)] * 2,
        compiler_params=pltpu.CompilerParams(vmem_limit_bytes=VMEM_LIMIT),
        cost_estimate=cost(4.8),
        name="early_out",
    )(place, mine, got)


def body(
    tokens_in, layer_norm_gain, layer_norm_bias, input_real, input_imag, decay_log, angle_log,
    scale_log, output_real, output_imag, skip_gain, glu_value, glu_gate, glu_bias, doc_lengths,
    out_grad
):
    rows_here, toks, width = tokens_in.shape
    n = input_real.shape[0]
    parts = lax.axis_size("seq")
    seat = lax.axis_index("seq")
    length = toks * parts
    hops = max(1, (length // 4) // toks)
    row_seat = lax.axis_index("rows")
    place = jnp.stack([seat * toks, row_seat % 2, row_seat // 2, seat]).astype(jnp.int32)
    rate = jnp.exp(decay_log)
    radius = jnp.exp(-rate)
    angle = jnp.exp(angle_log)
    cosine, sine = jnp.cos(angle), jnp.sin(angle)
    norm_root = jnp.sqrt(1.0 - jnp.exp(-2.0 * rate))
    scale = jnp.exp(scale_log) * norm_root
    lam = jnp.stack([radius * cosine, radius * sine])
    inputs = jnp.concatenate([input_real, input_imag], axis=0).astype(F32)
    scale2 = jnp.concatenate([scale, scale])
    scaled = (inputs * scale2[:, None]).astype(BF16)
    scale_b = jnp.broadcast_to(scale2[:, None], (2 * n, LANES))
    out_cat = jnp.concatenate([output_real, -output_imag], axis=1)
    gain, bias, skip = layer_norm_gain[None], layer_norm_bias[None], skip_gain[None]
    gbias = glu_bias[None]
    through = back_through = None
    if hops > 1:
        starts = jnp.cumsum(doc_lengths, axis=1) - doc_lengths - seat * toks
        clear = 1.0 - jnp.any((starts >= 0) & (starts < toks), axis=1).astype(F32)
        clear_next = 1.0 - jnp.any((starts >= 1) & (starts < toks + 1), axis=1).astype(F32)
        fr, fi = power_of(lam[0], lam[1], toks)
        through = clear[:, None, None] * jnp.concatenate([fr, fi])[None, None]
        back_through = clear_next[:, None, None] * jnp.concatenate([fr, -fi])[None, None]

    drive, xhat, rstd, ends, fin = run_forward(
        doc_lengths, place, tokens_in, gain, bias, scaled, lam
    )
    carry = carry_over(fin, through, "seq", parts, hops, False)
    block_out, gm, gs, st, bends, bfin, mine, send, gbias_g, sums = run_middle(
        doc_lengths, place, drive, ends, carry, xhat, tokens_in, out_grad, lam, out_cat, gain,
        bias, skip, glu_value, glu_gate, gbias
    )
    back_carry = carry_over(bfin, back_through, "seq", parts, hops, True)
    early = Exchange(place, mine, send, 0, "early")
    done = early.split(place)
    adj, mine_in, send_in = run_adjoint(
        doc_lengths, after(place, done), gs, bends, back_carry, st, xhat, lam, gbias_g, sums
    )
    late = Exchange(place, mine_in, send_in, EXTRA, "late")
    early.add_plane(after(early.own, adj))
    done = late.split(after(place, early.own))
    half_rows = rows_here // 2
    args = (adj, xhat, gm, out_grad, rstd, scaled, gain, skip)
    input_grad = run_input(doc_lengths, after(place, done), *args, 0, half_rows)
    late.add_plane(after(late.own, input_grad))
    early.add_line(after(early.own, late.own))
    input_grad = run_input(
        doc_lengths, after(place, early.own, late.own), *args, half_rows, rows_here, input_grad
    )
    late.add_line(after(late.own, input_grad))
    done = early.gather(after(place, late.own))
    done = late.gather(after(place, done))
    value_g, gate_g, real_g, imag_g = run_weights(
        after(place, done), early.mine, early.got[0], width, n
    )
    in_real_g, in_imag_g, small = glue(
        last_kernel,
        [SDS((n, width), F32), SDS((n, width), F32), SDS((SUBLANES, width), F32)],
        after(place, value_g), late.mine, late.got[0], late.own, scaled, input_real, input_imag,
        scale_b, gain, bias, skip, name="late_out",
    )
    gain_grad, shift_grad, skip_grad = small[0], small[1], small[2]
    scale_grad, lamg, gbias_g = small[3, :n], small[4], small[5:7].reshape(2 * width)
    lr, li = lamg[:n], lamg[n:]
    radius_grad = lr * cosine + li * sine
    angle_grad = radius * (li * cosine - lr * sine) * angle
    decay_grad = (
        -radius_grad * radius * rate
        + scale_grad * jnp.exp(scale_log) * jnp.exp(-2.0 * rate) * rate / norm_root
    )
    return (
        block_out, input_grad, gain_grad, shift_grad, in_real_g, in_imag_g, decay_grad,
        angle_grad, scale_grad * scale, real_g, imag_g, skip_grad, value_g, gate_g, gbias_g
    )


def solution(mesh):
    tokens = P("rows", "seq", None)
    placed = (tokens,) + (P(),) * 13 + (P("rows", None), tokens)
    return jax.shard_map(
        body, mesh=mesh, in_specs=placed, out_specs=(tokens, tokens) + (P(),) * 13,
        check_vma=False,
    )
```

```python
import functools

import jax
import jax.numpy as jnp
from jax import lax
from jax.experimental import pallas as pl
from jax.experimental.pallas import tpu as pltpu
from jax.sharding import PartitionSpec as P

EPSILON = 1e-05
SEGMENTS = 16
SUBLANES = 8
LANES = 128
EXTRA = 16
INPUT_BLOCK = 512
MIDDLE_CHUNK = 512
F32 = jnp.float32
BF16 = jnp.bfloat16
VMEM_LIMIT = 60 * 1024 * 1024
GLUE_LIMIT = 16 * 1024 * 1024
FULL_LIMIT = 67043328


def nt_dot(left, right):
    return lax.dot_general(
        left, right, (((1,), (1,)), ((), ())), preferred_element_type=F32
    )


def nn_dot(left, right):
    return lax.dot_general(
        left, right, (((1,), (0,)), ((), ())), preferred_element_type=F32
    )


def tn_dot(left, right):
    return lax.dot_general(
        left, right, (((0,), (0,)), ((), ())), preferred_element_type=F32
    )


def skewed_scan(step, inits, extra, span, reverse, ends=False):
    groups = SEGMENTS // SUBLANES
    per_group = len(inits) // groups
    seat = lax.broadcasted_iota(jnp.int32, (SUBLANES, LANES), 0)
    order = SUBLANES - 1 - seat if reverse else seat
    last = span + SUBLANES - 2

    def rows(i):
        base = last - i if reverse else i
        return [pl.ds(base + g * SUBLANES * span, SUBLANES, stride=span - 1) for g in range(groups)]

    states = list(inits)
    for i in range(SUBLANES):
        if i:
            states = [jnp.where(order == i, x, y) for x, y in zip(inits, states)]
        states, extra = step(rows(i), states, extra, order <= i)

    def body(i, carry):
        return step(rows(i), *carry, None)

    states, extra = lax.fori_loop(SUBLANES, span - 1, body, (states, extra), unroll=5)
    final = states
    for i in range(span - 1, last + 1):
        states, extra = step(rows(i), states, extra, order >= i - span + 1)
        if ends:
            final = [jnp.where(order == i - span + 1, x, y) for x, y in zip(states, final)]
    return final if ends else extra


def fill_keep(lens_ref, row, shift, keep, segs, span):
    toks = keep.shape[0]
    docs = lens_ref.shape[1]
    keep[...] = jnp.ones_like(keep)
    segs[...] = jnp.ones_like(segs)
    start = -shift
    for j in range(docs):

        @pl.when((start >= 0) & (start < toks))
        def _(start=start):
            keep[pl.ds(start, 1), :] = jnp.zeros((1, keep.shape[1]), F32)
            segs[pl.ds(start // span, 1), :] = jnp.zeros((1, segs.shape[1]), F32)

        start = start + lens_ref[row, j]


def power_of(real, imag, times):
    while times > 1:
        real, imag = real * real - imag * imag, 2.0 * real * imag
        times //= 2
    return real, imag


def to_blocks(work, part, value):
    for b in range(work.shape[0]):
        work[b, part, :] = value[:, b * LANES : (b + 1) * LANES]


def from_blocks(work, part):
    return jnp.concatenate([work[b, part, :] for b in range(work.shape[0])], axis=1)


def lane_blocks(vector, sign=1.0):
    n = vector.shape[1]
    return [
        jnp.broadcast_to(sign * vector[:, b * LANES : (b + 1) * LANES], (SUBLANES, LANES))
        for b in range(n // LANES)
    ]


def segment_ends(work, keep, real, imag, ends, span, reverse):
    groups = SEGMENTS // SUBLANES
    half = len(real)
    n = half * LANES
    zero = jnp.zeros((SUBLANES, LANES), F32)

    def step(rows, states, extra, live):
        out = []
        at = 0
        for g in range(groups):
            k = keep[rows[g], :]
            for b in range(half):
                sr, si = states[at], states[at + 1]
                at += 2
                ar, ai = k * real[b], k * imag[b]
                out.append((ar * sr + work[b, rows[g], :]) - ai * si)
                out.append((ar * si + work[half + b, rows[g], :]) + ai * sr)
        return out, extra

    final = skewed_scan(step, [zero] * (2 * groups * half), [], span, reverse, ends=True)
    at = 0
    for g in range(groups):
        for b in range(half):
            lanes = slice(b * LANES, (b + 1) * LANES)
            ends[g * SUBLANES : (g + 1) * SUBLANES, lanes] = final[at]
            lanes = slice(n + b * LANES, n + (b + 1) * LANES)
            ends[g * SUBLANES : (g + 1) * SUBLANES, lanes] = final[at + 1]
            at += 2


def starting_states(inits, half):
    n = half * LANES
    begin = []
    for g in range(SEGMENTS // SUBLANES):
        for b in range(half):
            for base in (0, n):
                lanes = slice(base + b * LANES, base + (b + 1) * LANES)
                begin.append(inits[g * SUBLANES : (g + 1) * SUBLANES, lanes])
    return begin


def compose_segments(ends, segs, real, imag, span, start_real, start_imag, inits, reverse):
    n = real.shape[1]
    pr, pi = power_of(real, imag, span)
    cr, ci = start_real, start_imag
    order = range(SEGMENTS - 1, -1, -1) if reverse else range(SEGMENTS)
    for s in order:
        if inits is not None:
            inits[s : s + 1, 0:n] = cr
            inits[s : s + 1, n : 2 * n] = ci
        k = segs[s : s + 1, :]
        ar, ai = k * pr, k * pi
        er, ei = ends[s : s + 1, 0:n], ends[s : s + 1, n : 2 * n]
        cr, ci = (ar * cr + er) - ai * ci, (ar * ci + ei) + ai * cr
    return cr, ci


def forward_kernel(
    lens, x_ref, gain, bias, scaled, lam, drive_ref, xhat_ref, rstd_ref, ends_ref,
    fin_ref, work, keep, segs
):
    row = pl.program_id(0)
    toks = x_ref.shape[1]
    n = lam.shape[1]
    span = toks // SEGMENTS
    fill_keep(lens, row, lax.axis_index("seq") * toks, keep, segs, span)
    chunk = 256
    for c in range(toks // chunk):
        part = slice(c * chunk, (c + 1) * chunk)
        x = x_ref[0, part, :].astype(F32)
        cent = x - jnp.mean(x, axis=-1, keepdims=True)
        rstd = lax.rsqrt(jnp.mean(cent * cent, axis=-1, keepdims=True) + EPSILON)
        xhat = cent * rstd
        rstd_ref[0, part, :] = jnp.broadcast_to(rstd, (chunk, rstd_ref.shape[2]))
        xhat_ref[0, part, :] = xhat.astype(BF16)
        low = (xhat * gain[...] + bias[...]).astype(BF16)
        drive = nt_dot(low, scaled[...]).astype(BF16)
        drive_ref[0, part, :] = drive
        to_blocks(work, part, drive.astype(F32))
    real, imag = lam[6:7, :], lam[7:8, :]
    ends = ends_ref.at[0]
    segment_ends(work, keep, lane_blocks(real), lane_blocks(imag), ends, span, False)
    zero = jnp.zeros((1, n), F32)
    cr, ci = compose_segments(ends, segs, real, imag, span, zero, zero, None, False)
    fin_ref[0, :, 0:n] = cr
    fin_ref[0, :, n : 2 * n] = ci


LOG2E = 1.4426950408889634
TAIL_P = 0.3275911 * 0.7071067811865476
TAIL = (0.254829592, -0.284496736, 1.421413741, -1.453152027, 1.061405429)


def gelu_parts(m):
    bell = jnp.exp2((-0.5 * LOG2E) * (m * m))
    t = 1.0 / (1.0 + TAIL_P * jnp.abs(m))
    poly = t * (0.5 * TAIL[0] + t * (0.5 * TAIL[1] + t * (0.5 * TAIL[2] + t * (0.5 * TAIL[3] + t * (0.5 * TAIL[4])))))
    tail = poly * bell
    return jnp.where(m < 0, tail, 1.0 - tail), bell


def middle_kernel(
    lens, first, drive_ref, ends_ref, carry_ref, xhat_ref, x_ref, og_ref, lam, out_cat, gain,
    bias, skip, wv_ref, wg_ref, gbias, block_ref, gm_ref, gs_ref, st_ref, bends_ref, bfin_ref, mine_ref,
    send_ref, gbias_ref, sums_ref, work, keep, segs, done, inits, act_s, gvg_s, acc
):
    row = pl.program_id(0)
    toks, width = x_ref.shape[1], x_ref.shape[2]
    n = lam.shape[1]
    span = toks // SEGMENTS
    groups = SEGMENTS // SUBLANES

    @pl.when(row == 0)
    def _():
        acc[...] = jnp.zeros_like(acc)
        gbias_ref[...] = jnp.zeros_like(gbias_ref)
        sums_ref[...] = jnp.zeros_like(sums_ref)

    fill_keep(lens, row, first[0], keep, segs, span)
    everything = slice(0, toks)
    to_blocks(work, everything, drive_ref[0].astype(F32))
    real, imag = lam[6:7, :], lam[7:8, :]
    half = n // LANES
    real_b, imag_b = lane_blocks(real), lane_blocks(imag)
    compose_segments(
        ends_ref.at[0], segs, real, imag, span, carry_ref[0, :, 0:n],
        carry_ref[0, :, n : 2 * n], inits, False
    )

    def step(rows, states, extra, live):
        out = []
        at = 0
        for g in range(groups):
            k = keep[rows[g], :]
            for b in range(half):
                sr, si = states[at], states[at + 1]
                at += 2
                ar, ai = k * real_b[b], k * imag_b[b]
                nr = (ar * sr + work[b, rows[g], :]) - ai * si
                ni = (ar * si + work[half + b, rows[g], :]) + ai * sr
                done[b, rows[g], :] = nr
                done[half + b, rows[g], :] = ni
                out += [nr, ni]
        return out, extra

    skewed_scan(step, starting_states(inits, half), [], span, False)

    docs = lens.shape[1]
    limit = -first[0]
    for j in range(docs - 1):
        limit = limit + lens[row, j]
    chunk = MIDDLE_CHUNK
    mix_gain, mix_bias = gain[...] * skip[...], bias[...] * skip[...]
    half_bias = 0.5 * gbias[...]
    wv, wg = wv_ref[...] * BF16(0.5), wg_ref[...] * BF16(0.5)
    for c in range(toks // chunk):
        part = slice(c * chunk, (c + 1) * chunk)
        state = from_blocks(done, part).astype(BF16)
        st_ref[0, part, :] = state
        xhat = xhat_ref[0, part, :].astype(F32)
        mixed = nt_dot(state, out_cat[...]) + (xhat * mix_gain + mix_bias)
        cdf, bell = gelu_parts(mixed)
        act = (mixed * cdf).astype(BF16)
        act_s[part, :] = act
        slope = cdf + mixed * (bell * 0.3989422804014327)
        value = nn_dot(act, wv) + half_bias[:, 0:width]
        tanh = jnp.tanh(nn_dot(act, wg) + half_bias[:, width : 2 * width])
        u = 1.0 + tanh
        gated = value * u
        block_ref[0, part, :] = (x_ref[0, part, :].astype(F32) + gated).astype(BF16)
        place = lax.broadcasted_iota(jnp.int32, (chunk, width), 0) + c * chunk
        grad = jnp.where(place < limit, og_ref[0, part, :].astype(F32), 0.0)
        gv = grad * u
        gg = grad * gated * (1.0 - tanh)
        gbias_ref[0:1, 0:width] += jnp.sum(gv, axis=0, keepdims=True)
        gbias_ref[0:1, width : 2 * width] += jnp.sum(gg, axis=0, keepdims=True)
        gv, gg = gv.astype(BF16), gg.astype(BF16)
        gvg_s[part, 0:width] = gv
        gvg_s[part, width : 2 * width] = gg
        gm = (nt_dot(gv, wv) + nt_dot(gg, wg)) * slope
        sums_ref[0:1, :] += jnp.sum(gm, axis=0, keepdims=True)
        sums_ref[1:2, :] += jnp.sum(gm * xhat, axis=0, keepdims=True)
        gm = gm.astype(BF16)
        gm_ref[0, part, :] = gm
        gs = nn_dot(gm, out_cat[...])
        gs_ref[0, part, :] = gs.astype(BF16)
        to_blocks(work, part, gs)
    acc[:, 0 : 2 * width] += tn_dot(act_s[...], gvg_s[...])
    acc[:, 2 * width :] += tn_dot(gm_ref[0], st_ref[0])
    fill_keep(lens, row, first[0] + 1, keep, segs, span)
    bends = bends_ref.at[0]
    segment_ends(work, keep, real_b, lane_blocks(imag, -1.0), bends, span, True)
    zero = jnp.zeros((1, n), F32)
    cr, ci = compose_segments(bends, segs, real, -imag, span, zero, zero, None, True)
    bfin_ref[0, :, 0:n] = cr
    bfin_ref[0, :, n : 2 * n] = ci

    @pl.when(row == pl.num_programs(0) - 1)
    def _():
        acc[:, 0 : 2 * width] = 0.5 * acc[:, 0 : 2 * width]
        gbias_ref[...] = 0.5 * gbias_ref[...]
        split_halves(acc, first[1], mine_ref, send_ref)


def split_halves(acc, core, mine_ref, send_ref):
    half = acc.shape[0] // 2
    mine_ref[0:half, :] = acc[pl.ds(pl.multiple_of(core * half, half), half), :].astype(BF16)
    send_ref[0:half, :] = acc[pl.ds(pl.multiple_of((1 - core) * half, half), half), :].astype(BF16)


def put_pair(vec, ref, at):
    high = vec.astype(BF16)
    low = (vec - high.astype(F32)).astype(BF16)
    ref[at : at + 2 * SUBLANES, :] = jnp.concatenate([high, low], axis=0)


def get_pair(ref, at):
    return (
        ref[at : at + SUBLANES, :].astype(F32)
        + ref[at + SUBLANES : at + 2 * SUBLANES, :].astype(F32)
    )


def adjoint_kernel(
    lens, first, gs_ref, bends_ref, carry_ref, st_ref, xhat_ref, lam, gbias_ref, sums_ref, adj_ref,
    mine_ref, send_ref, state, work, keep, segs, done, inits, acc, tots
):
    row = pl.program_id(0)
    toks, width = xhat_ref.shape[1], xhat_ref.shape[2]
    n = lam.shape[1]
    span = toks // SEGMENTS
    groups = SEGMENTS // SUBLANES

    @pl.when(row == 0)
    def _():
        acc[...] = jnp.zeros_like(acc)
        tots[...] = jnp.zeros_like(tots)

    fill_keep(lens, row, first[0] + 1, keep, segs, span)
    everything = slice(0, toks)
    to_blocks(work, everything, gs_ref[0].astype(F32))
    to_blocks(state, everything, st_ref[0].astype(F32))
    real, imag = lam[6:7, :], -lam[7:8, :]
    half = n // LANES
    real_b, imag_b = lane_blocks(real), lane_blocks(imag)
    compose_segments(
        bends_ref.at[0], segs, real, imag, span, carry_ref[0, :, 0:n],
        carry_ref[0, :, n : 2 * n], inits, True
    )

    def step(rows, states, tot, live):
        out = []
        tot = list(tot)
        at = 0
        for g in range(groups):
            k = keep[rows[g], :]
            for b in range(half):
                sr, si = states[at], states[at + 1]
                at += 2
                ur, ui = k * sr, k * si
                nr = (real_b[b] * ur + work[b, rows[g], :]) - imag_b[b] * ui
                ni = (real_b[b] * ui + work[half + b, rows[g], :]) + imag_b[b] * ur
                done[b, rows[g], :] = nr
                done[half + b, rows[g], :] = ni
                out += [nr, ni]
                hr, hi = state[b, rows[g], :], state[half + b, rows[g], :]
                if live is not None:
                    ur, ui, nr, ni = (jnp.where(live, v, 0.0) for v in (ur, ui, nr, ni))
                tot[4 * b] = tot[4 * b] + (ur * hr + ui * hi)
                tot[4 * b + 1] = tot[4 * b + 1] + (ui * hr - ur * hi)
                tot[4 * b + 2] = tot[4 * b + 2] + nr
                tot[4 * b + 3] = tot[4 * b + 3] + ni
        return out, tot

    zero8 = jnp.zeros((SUBLANES, LANES), F32)
    tot = skewed_scan(step, starting_states(inits, half), [zero8] * (4 * half), span, True)
    for b in range(half):
        low_lanes = slice(b * LANES, (b + 1) * LANES)
        high_lanes = slice(n + b * LANES, n + (b + 1) * LANES)
        tots[0, :, low_lanes] += tot[4 * b]
        tots[0, :, high_lanes] += tot[4 * b + 1]
        tots[1, :, low_lanes] += tot[4 * b + 2]
        tots[1, :, high_lanes] += tot[4 * b + 3]

    adj = from_blocks(done, everything).astype(BF16)
    adj_ref[0] = adj
    acc[...] += tn_dot(adj, xhat_ref[0])

    @pl.when(row == pl.num_programs(0) - 1)
    def _():
        split_halves(acc, first[1], mine_ref, send_ref)
        vec = jnp.concatenate(
            [gbias_ref[:, 0:width], gbias_ref[:, width : 2 * width], sums_ref[...],
             jnp.sum(tots[0], axis=0, keepdims=True), jnp.sum(tots[1], axis=0, keepdims=True),
             jnp.zeros((2, width), F32)], axis=0
        )
        put_pair(vec, mine_ref, n)
        put_pair(vec, send_ref, n)


def input_kernel(
    begin, lens, first, adj_ref, xhat_ref, gm_ref, og_ref, rstd_ref, scaled, gain, skip, *refs
):
    ig_ref = refs[-1]
    row = pl.program_id(0) + begin
    tall, width = xhat_ref.shape[1], xhat_ref.shape[2]
    limit = -first[0] - pl.program_id(1) * tall
    for j in range(lens.shape[1] - 1):
        limit = limit + lens[row, j]
    xhat = xhat_ref[0].astype(F32)
    g = nn_dot(adj_ref[0], scaled[...]) * gain[...]
    g = g + gm_ref[0].astype(F32) * (gain[...] * skip[...])
    place = lax.broadcasted_iota(jnp.int32, (tall, width), 0)
    grad = jnp.where(place < limit, og_ref[0].astype(F32), 0.0)
    m1 = jnp.mean(g, axis=-1, keepdims=True)
    m2 = jnp.mean(g * xhat, axis=-1, keepdims=True)
    ig_ref[0] = (grad + rstd_ref[0, :, 0:1] * (g - m1 - xhat * m2)).astype(BF16)


def tree_sum(items):
    while len(items) > 1:
        items = [items[i] + items[i + 1] for i in range(0, len(items), 2)]
    return items[0]


def split_kernel(extra, bits, place, mine_ref, got_ref, *refs):
    half = mine_ref.shape[0] - extra
    piece = refs[0].shape[0] - extra
    own = seat_of(place, bits)

    def part(index):
        rows = pl.ds(pl.multiple_of(index * piece, piece), piece)
        return mine_ref[rows, :].astype(F32) + got_ref[rows, :].astype(F32)

    for j, ref in enumerate(refs):
        ref[0:piece, :] = part(own ^ j).astype(BF16)
    if extra:
        vec = get_pair(mine_ref, half) + get_pair(got_ref, half)
        for ref in refs:
            put_pair(vec, ref, piece)


def seat_of(place, bits):
    low, high = bits
    index = place[1 + low]
    for k in range(low + 1, high):
        index = index + (place[1 + k] << (k - low))
    return index


def sum_kernel(extra, *refs):
    out = refs[-1]
    rows = out.shape[0] - extra
    out[0:rows, :] = tree_sum([r[0:rows, :].astype(F32) for r in refs[:-1]]).astype(BF16)
    if extra:
        put_pair(tree_sum([get_pair(r, rows) for r in refs[:-1]]), out, rows)


def gather_kernel(bits, place, *refs):
    out_ref = refs[-1]
    count = len(refs) - 1
    piece = out_ref.shape[0] // count
    own = seat_of(place, bits)
    for j, ref in enumerate(refs[:-1]):
        rows = pl.ds(pl.multiple_of((own ^ j) * piece, piece), piece)
        out_ref[rows, :] = ref[0:piece, :]


def weights_kernel(place, mine_ref, got_ref, value_ref, gate_ref, real_ref, imag_ref):
    width = value_ref.shape[1]
    n = real_ref.shape[1]

    def put(ref):
        value_ref[...] = ref[:, 0:width].astype(F32)
        gate_ref[...] = ref[:, width : 2 * width].astype(F32)
        real_ref[...] = ref[:, 2 * width : 2 * width + n].astype(F32)
        imag_ref[...] = -ref[:, 2 * width + n :].astype(F32)

    @pl.when(pl.program_id(0) == 0)
    def _():
        put(mine_ref)

    @pl.when(pl.program_id(0) == 1)
    def _():
        put(got_ref)


def last_kernel(
    place, mine_ref, got_ref, own_ref, scaled_ref, real_ref, imag_ref, coef, gain, bias, skip,
    real_out, imag_out, gain_out, shift_out, skip_out, decay_out, angle_out, scale_out, gbias_out
):
    n, width = real_ref.shape
    vec = get_pair(own_ref, own_ref.shape[0] - 2 * SUBLANES)
    sum_gm, sum_gmx = vec[2:3, :], vec[3:4, :]
    col = jnp.transpose(vec)[:, 5:6]
    scale = jnp.transpose(coef[...])[:, 5:6]
    gain_sum = skip[...] * sum_gmx
    shift = skip[...] * sum_gm
    first_core = place[1] == 0
    scale_sums = jnp.zeros((n, 1), F32)
    for part, weight_ref, out_ref in ((0, real_ref, real_out), (1, imag_ref, imag_out)):
        rows = slice(part * n, (part + 1) * n)
        keep_mine = first_core if part == 0 else jnp.logical_not(first_core)
        total = jnp.where(keep_mine, mine_ref[...], got_ref[...]).astype(F32)
        scaled = scaled_ref[rows, :].astype(F32)
        gain_sum = gain_sum + jnp.sum(total * scaled, axis=0, keepdims=True)
        shift = shift + jnp.sum(col[rows, :] * scaled, axis=0, keepdims=True)
        full = total * gain[...] + col[rows, :] * bias[...]
        out_ref[...] = full * scale
        scale_sums = scale_sums + jnp.sum(
            full * weight_ref[...].astype(F32), axis=1, keepdims=True
        )
    scale_grad = jnp.transpose(jnp.broadcast_to(scale_sums, (n, LANES)))[0:1, :]
    lr, li = vec[4:5, 0:n], vec[4:5, n : 2 * n]
    radius_grad = lr * coef[0:1, :] + li * coef[1:2, :]
    gain_out[...] = gain_sum.reshape(width)
    shift_out[...] = shift.reshape(width)
    skip_out[...] = (gain[...] * sum_gmx + bias[...] * sum_gm).reshape(width)
    decay_out[...] = (scale_grad * coef[4:5, :] - radius_grad * coef[3:4, :]).reshape(n)
    angle_out[...] = (coef[2:3, :] * (li * coef[0:1, :] - lr * coef[1:2, :])).reshape(n)
    scale_out[...] = (scale_grad * coef[5:6, :]).reshape(n)
    gbias_out[0:width] = vec[0, :]
    gbias_out[width : 2 * width] = vec[1, :]


def prepare_kernel(
    decay_log, angle_log, scale_log, real_ref, imag_ref, out_real, out_imag, coef, scaled_ref, out_cat
):
    n = real_ref.shape[0]
    rate = jnp.exp(decay_log[...])
    radius = jnp.exp(-rate)
    angle = jnp.exp(angle_log[...])
    cosine, sine = jnp.cos(angle), jnp.sin(angle)
    shrink = jnp.exp(-2.0 * rate)
    root = jnp.sqrt(1.0 - shrink)
    grown = jnp.exp(scale_log[...])
    scale = grown * root
    rows = (cosine, sine, radius * angle, radius * rate, grown * shrink * rate / root, scale,
            radius * cosine, radius * sine)
    for i, row in enumerate(rows):
        coef[i : i + 1, :] = row
    column = jnp.transpose(coef[...])[:, 5:6]
    scaled_ref[0:n, :] = (real_ref[...].astype(F32) * column).astype(BF16)
    scaled_ref[n : 2 * n, :] = (imag_ref[...].astype(F32) * column).astype(BF16)
    out_cat[:, 0:n] = out_real[...]
    out_cat[:, n : 2 * n] = -out_imag[...]


def whole(shape):
    return pl.BlockSpec(shape, lambda r: (0,) * len(shape))


def per_row(*shape):
    return pl.BlockSpec((1,) + shape, lambda r: (r,) + (0,) * len(shape))


SCALARS = pl.BlockSpec(memory_space=pltpu.SMEM)


def carry_over(fin, through, axis, parts, hops, reverse):
    def shift(v):
        pairs = [(i, i + 1) for i in range(parts - 1)]
        if reverse:
            pairs = [(b, a) for a, b in pairs]
        return lax.ppermute(v, axis, pairs)

    if hops == 1:
        return shift(fin)
    n = fin.shape[-1] // 2
    total = shift(fin)
    for _ in range(hops - 1):
        tr, ti = through[..., :n], through[..., n:]
        sr, si = total[..., :n], total[..., n:]
        passed = jnp.concatenate([tr * sr - ti * si, tr * si + ti * sr], axis=-1)
        total = shift(fin + passed)
    return total


def glue(kernel, outs, *args, name, scalars=True, grant=GLUE_LIMIT):
    def spec(v):
        return pl.BlockSpec(v.shape, lambda i: (0,) * len(v.shape))

    specs = [SCALARS] * scalars + [spec(v) for v in args[scalars:]]
    many = isinstance(outs, list)
    return pl.pallas_call(
        kernel, grid=(1,), in_specs=specs, out_specs=[spec(v) for v in outs] if many else spec(outs),
        out_shape=outs, cost_estimate=cost(1.7),
        compiler_params=pltpu.CompilerParams(vmem_limit_bytes=grant), name=name,
    )(*args)


def from_row(v, offset):
    count = lax.axis_size("rows")
    return lax.ppermute(v, "rows", [(i, i ^ offset) for i in range(count)])


def from_line(v, offset):
    return lax.ppermute(v, "seq", [(i, i ^ offset) for i in range(lax.axis_size("seq"))])


def after(v, *others):
    return lax.optimization_barrier((v,) + others)[0]


class Exchange:
    def __init__(self, mine, send, extra, stages, name, hops):
        self.mine, self.extra, self.stages, self.name = mine, extra, stages, name
        self.hops = hops
        self.cut, self.back = 0, len(stages) - 1
        self.got = [from_row(send, 1)]

    def rows(self, count):
        return SDS((count, self.mine.shape[1]), BF16)

    def split(self, place):
        self.cut += 1
        bits = self.stages[self.cut]
        pieces = 1 << (bits[1] - bits[0])
        piece = (self.mine.shape[0] - self.extra) // pieces + self.extra
        self.mine, *cuts = glue(
            functools.partial(split_kernel, self.extra, bits), [self.rows(piece)] * pieces, place,
            self.mine, *self.got, name=self.name + "_split"
        )
        self.got = [from_row(c, (j + 1) << bits[0]) for j, c in enumerate(cuts)]
        return self.mine

    def add(self, place):
        self.mine = glue(
            drop_place(functools.partial(sum_kernel, self.extra)), self.rows(self.mine.shape[0]),
            place, self.mine, *self.got, name=self.name + "_sum"
        )
        if self.hops:
            offsets, *self.hops = self.hops
            self.got = [from_line(self.mine, j) for j in offsets]
            return self.mine
        self.total = self.mine
        if self.extra:
            self.mine = self.mine[: self.mine.shape[0] - self.extra]
        self.send_back()
        return self.total

    def send_back(self):
        low, high = self.stages[self.back]
        self.got = [from_row(self.mine, j << low) for j in range(1, 1 << (high - low))]

    def gather(self, place):
        bits = self.stages[self.back]
        pieces = [self.mine] + self.got
        self.mine = glue(
            functools.partial(gather_kernel, bits), self.rows(len(pieces) * self.mine.shape[0]),
            place, *pieces, name=self.name + "_gather"
        )
        self.back -= 1
        self.send_back()
        return self.mine


def drop_place(kernel):
    def call(place, *refs):
        kernel(*refs)

    return call


def cost(us):
    return pl.CostEstimate(flops=int(us * 1e9), bytes_accessed=1 << 20, transcendentals=0)


PARAMS = pltpu.CompilerParams(
    dimension_semantics=("arbitrary",), vmem_limit_bytes=VMEM_LIMIT
)
SDS = jax.ShapeDtypeStruct


def scan_scratch(toks, n):
    return [
        pltpu.VMEM((2 * n // LANES, toks, LANES), F32), pltpu.VMEM((toks, LANES), F32),
        pltpu.VMEM((SEGMENTS, n), F32),
    ]


def run_forward(lens, x, gain, bias, scaled, lam):
    rows_here, toks, width = x.shape
    n = lam.shape[1]
    act = per_row(toks, width)
    return pl.pallas_call(
        forward_kernel,
        grid=(rows_here,),
        in_specs=[SCALARS, act, whole((1, width)), whole((1, width)),
                  whole((2 * n, width)), whole((8, n))],
        out_specs=[per_row(toks, 2 * n), act, per_row(toks, 128), per_row(SEGMENTS, 2 * n),
                   per_row(1, 2 * n)],
        out_shape=[SDS((rows_here, toks, 2 * n), BF16), SDS(x.shape, BF16),
                   SDS((rows_here, toks, 128), F32), SDS((rows_here, SEGMENTS, 2 * n), F32),
                   SDS((rows_here, 1, 2 * n), F32)],
        scratch_shapes=scan_scratch(toks, n),
        compiler_params=PARAMS,
        cost_estimate=cost(10.6),
        name="forward",
    )(lens, x, gain, bias, scaled, lam)


def run_middle(
    lens, place, drive, ends, carry, xhat, x, og, lam, out_cat, gain, bias, skip, wv, wg, gbias
):
    rows_here, toks, width = x.shape
    n = lam.shape[1]
    cols = 2 * width + 2 * n
    act, chan = per_row(toks, width), per_row(toks, 2 * n)
    return pl.pallas_call(
        middle_kernel,
        grid=(rows_here,),
        in_specs=[SCALARS, SCALARS, chan, per_row(SEGMENTS, 2 * n),
                  per_row(1, 2 * n), act, act, act, whole((8, n)), whole((width, 2 * n)),
                  whole((1, width)), whole((1, width)), whole((1, width)),
                  whole((width, width)), whole((width, width)), whole((1, 2 * width))],
        out_specs=[act, act, chan, chan, per_row(SEGMENTS, 2 * n), per_row(1, 2 * n),
                   whole((width // 2, cols)), whole((width // 2, cols)), whole((1, 2 * width)),
                   whole((2, width))],
        out_shape=[SDS(x.shape, BF16), SDS(x.shape, BF16), SDS((rows_here, toks, 2 * n), BF16),
                   SDS((rows_here, toks, 2 * n), BF16), SDS((rows_here, SEGMENTS, 2 * n), F32),
                   SDS((rows_here, 1, 2 * n), F32), SDS((width // 2, cols), BF16),
                   SDS((width // 2, cols), BF16), SDS((1, 2 * width), F32),
                   SDS((2, width), F32)],
        scratch_shapes=scan_scratch(toks, n) + [
            pltpu.VMEM((2 * n // LANES, toks, LANES), F32), pltpu.VMEM((SEGMENTS, 2 * n), F32),
            pltpu.VMEM((toks, width), BF16), pltpu.VMEM((toks, 2 * width), BF16),
            pltpu.VMEM((width, cols), F32)],
        compiler_params=PARAMS,
        cost_estimate=cost(48),
        name="middle",
    )(lens, place, drive, ends, carry, xhat, x, og, lam, out_cat, gain, bias, skip, wv, wg, gbias)


def run_adjoint(lens, place, gs, bends, carry, st, xhat, lam, gbias_g, sums):
    rows_here, toks, width = xhat.shape
    n = lam.shape[1]
    act, chan = per_row(toks, width), per_row(toks, 2 * n)
    return pl.pallas_call(
        adjoint_kernel,
        grid=(rows_here,),
        in_specs=[SCALARS, SCALARS, chan, per_row(SEGMENTS, 2 * n), per_row(1, 2 * n), chan, act,
                  whole((8, n)), whole((1, 2 * width)), whole((2, width))],
        out_specs=[chan, whole((n + EXTRA, width)), whole((n + EXTRA, width))],
        out_shape=[SDS((rows_here, toks, 2 * n), BF16), SDS((n + EXTRA, width), BF16),
                   SDS((n + EXTRA, width), BF16)],
        scratch_shapes=[pltpu.VMEM((2 * n // LANES, toks, LANES), F32)] + scan_scratch(toks, n) + [
            pltpu.VMEM((2 * n // LANES, toks, LANES), F32), pltpu.VMEM((SEGMENTS, 2 * n), F32),
            pltpu.VMEM((2 * n, width), F32),
            pltpu.VMEM((2, SUBLANES, 2 * n), F32)],
        compiler_params=PARAMS,
        cost_estimate=cost(12),
        name="adjoint",
    )(lens, place, gs, bends, carry, st, xhat, lam, gbias_g, sums)


def run_input(lens, place, adj, xhat, gm, og, rstd, scaled, gain, skip, begin=0, end=None, into=None):
    rows_here, toks, width = xhat.shape
    end = rows_here if end is None else end

    tall = INPUT_BLOCK

    def rows(_, lanes):
        return pl.BlockSpec((1, tall, lanes), lambda r, t: (r + begin if begin else r, t, 0))

    def fixed(shape):
        return pl.BlockSpec(shape, lambda r, t: (0,) * len(shape))

    act = rows(toks, width)
    args = (lens, place, adj, xhat, gm, og, rstd, scaled, gain, skip)
    specs = [SCALARS, SCALARS, rows(toks, adj.shape[2]), act, act, act,
             rows(toks, 128), fixed(scaled.shape), fixed((1, width)), fixed((1, width))]
    if into is not None:
        args, specs = args + (into,), specs + [pl.BlockSpec(memory_space=pl.ANY)]
    return pl.pallas_call(
        functools.partial(input_kernel, begin),
        grid=(end - begin, toks // tall),
        in_specs=specs,
        out_specs=act,
        out_shape=SDS(xhat.shape, BF16),
        input_output_aliases={} if into is None else {len(args) - 1: 0},
        compiler_params=pltpu.CompilerParams(vmem_limit_bytes=VMEM_LIMIT),
        cost_estimate=cost(8),
        name="input",
    )(*args)


def run_weights(place, mine, got, width, n):
    half, cols = mine.shape
    blocks = 1
    tall = half // blocks
    mine_spec = pl.BlockSpec((tall, cols), lambda p, i, place: (jnp.where(p == 0, i, blocks - 1), 0))
    got_spec = pl.BlockSpec((tall, cols), lambda p, i, place: (jnp.where(p == 0, 0, i), 0))

    def out(c):
        return pl.BlockSpec((tall, c), lambda p, i, place: ((place[1] ^ p) * blocks + i, 0))

    return pl.pallas_call(
        weights_kernel,
        grid_spec=pltpu.PrefetchScalarGridSpec(
            num_scalar_prefetch=1, grid=(2, blocks), in_specs=[mine_spec, got_spec],
            out_specs=[out(width), out(width), out(n), out(n)],
        ),
        out_shape=[SDS((2 * half, width), F32)] * 2 + [SDS((2 * half, n), F32)] * 2,
        compiler_params=pltpu.CompilerParams(vmem_limit_bytes=VMEM_LIMIT),
        cost_estimate=cost(4.8),
        name="early_out",
    )(place, mine, got)


ORDER = (
    "early_split",
    "adjoint",
    "early_add",
    "late_split",
    "input0",
    "late_add",
    "early_add",
    "input1",
    "late_add",
    "early_gather",
    "late_gather",
    "early_out",
)


def body(
    tokens_in, layer_norm_gain, layer_norm_bias, input_real, input_imag, decay_log, angle_log,
    scale_log, output_real, output_imag, skip_gain, glu_value, glu_gate, glu_bias, doc_lengths,
    out_grad
):
    rows_here, toks, width = tokens_in.shape
    n = input_real.shape[0]
    parts = lax.axis_size("seq")
    seat = lax.axis_index("seq")
    length = toks * parts
    hops = max(1, (length // 4) // toks)
    row_seat = lax.axis_index("rows")
    seat_bits = lax.axis_size("rows").bit_length() - 1
    place = jnp.stack(
        [seat * toks] + [(row_seat >> k) & 1 for k in range(seat_bits)]
    ).astype(jnp.int32)
    coef, scaled, out_cat = glue(
        prepare_kernel,
        [SDS((8, n), F32), SDS((2 * n, width), BF16), SDS((width, 2 * n), BF16)],
        decay_log[None], angle_log[None], scale_log[None], input_real, input_imag, output_real,
        output_imag, name="prepare", scalars=False, grant=FULL_LIMIT
    )
    gain, bias, skip = layer_norm_gain[None], layer_norm_bias[None], skip_gain[None]
    gbias = glu_bias[None]
    through = back_through = None
    if hops > 1:
        starts = jnp.cumsum(doc_lengths, axis=1) - doc_lengths - seat * toks
        clear = 1.0 - jnp.any((starts >= 0) & (starts < toks), axis=1).astype(F32)
        clear_next = 1.0 - jnp.any((starts >= 1) & (starts < toks + 1), axis=1).astype(F32)
        fr, fi = power_of(coef[6], coef[7], toks)
        through = clear[:, None, None] * jnp.concatenate([fr, fi])[None, None]
        back_through = clear_next[:, None, None] * jnp.concatenate([fr, -fi])[None, None]

    drive, xhat, rstd, ends, fin = run_forward(
        doc_lengths, tokens_in, gain, bias, scaled, coef
    )
    carry = carry_over(fin, through, "seq", parts, hops, False)
    block_out, gm, gs, st, bends, bfin, mine, send, gbias_g, sums = run_middle(
        doc_lengths, place, drive, ends, carry, xhat, tokens_in, out_grad, coef, out_cat, gain,
        bias, skip, glu_value, glu_gate, gbias
    )
    back_carry = carry_over(bfin, back_through, "seq", parts, hops, True)
    stages = [(0, 1), (1, seat_bits)]
    doubling = [[1 << k] for k in range(parts.bit_length() - 1)]
    at_once = [list(range(1, parts))]
    early = Exchange(mine, send, 0, stages, "early", at_once)
    late = input_grad = None
    done = place
    half_rows = rows_here // 2
    for task in ORDER:
        now = after(place, done)
        if task == "adjoint":
            adj, mine_in, send_in = run_adjoint(
                doc_lengths, now, gs, bends, back_carry, st, xhat, coef, gbias_g, sums
            )
            late = Exchange(mine_in, send_in, EXTRA, stages, "late", at_once)
            done = adj
        elif task in ("input0", "input1"):
            begin = 0 if input_grad is None else half_rows
            input_grad = done = run_input(
                doc_lengths, now, adj, xhat, gm, out_grad, rstd, scaled, gain, skip, begin,
                begin + half_rows, input_grad
            )
        elif task == "early_out":
            value_g, gate_g, real_g, imag_g = run_weights(now, early.mine, early.got[0], width, n)
            done = value_g
        else:
            which, step = task.split("_")
            done = getattr(early if which == "early" else late, step)(now)
    in_real_g, in_imag_g, *vectors = glue(
        last_kernel,
        [SDS((n, width), F32)] * 2 + [SDS((width,), F32)] * 3 + [SDS((n,), F32)] * 3
        + [SDS((2 * width,), F32)],
        after(place, done), late.mine, late.got[0], late.total, scaled, input_real, input_imag,
        coef, gain, bias, skip, name="late_out",
    )
    gain_grad, shift_grad, skip_grad, decay_grad, angle_grad, scale_grad, gbias_g = vectors
    return (
        block_out, input_grad, gain_grad, shift_grad, in_real_g, in_imag_g, decay_grad,
        angle_grad, scale_grad, real_g, imag_g, skip_grad, value_g, gate_g, gbias_g
    )


def solution(mesh):
    tokens = P("rows", "seq", None)
    placed = (tokens,) + (P(),) * 13 + (P("rows", None), tokens)
    return jax.shard_map(
        body, mesh=mesh, in_specs=placed, out_specs=(tokens, tokens) + (P(),) * 13,
        check_vma=False,
    )
```
